32 devices in a mesh: slab: 8 (over y, x, core), grp: 4 (over z).
Axes of the slice: x: 2, y: 2, z: 4, core: 2. Of those that a mesh axis runs over, the one named last changes fastest.
Arguments:
- pressure: float32 [64, 512, 256], P('slab', 'grp'), may hold values from -6 to 6
- velocity: float32 [3, 64, 512, 256], P(None, 'slab', 'grp'), may hold values from -6 to 6
- stiffness: float32 [64, 512, 256], P('slab', 'grp'), may hold values from 1 to 2.5
- buoyancy: float32 [64, 512, 256], P('slab', 'grp'), may hold values from 0.5 to 1
- traces: bfloat16 [1024, 128], P(('slab', 'grp')), may hold values from -6 to 6
- lateral: bfloat16 [1024, 2, 8], P(('slab', 'grp')), may hold values from -1 to 1
- routes: int32 [1024, 2], replicated, may hold values from 0 to 7, all different within a row; in each aligned block of 32 rows (0 to 31, 32 to 63, ...) at most 8 rows name the same one
- ycenter: int32 [1024], replicated, may hold values from 0 to 511
Outputs:
- pressure_out: float32 [64, 512, 256], P('slab', 'grp')
- velocity_out: float32 [3, 64, 512, 256], P(None, 'slab', 'grp')
The draws below stay inside these ranges and needn't reach their ends.
Inputs may be any that keep to these rules, and one draw needn't show every extreme that they name: `routes`: each sensor lists 2 different slabs; among the 32 sensors held by one device no slab is listed more than 8 times, a bound that some block reaches.
All inputs are finite; a program needn't handle non-finite values.
Results may differ from the reference program's by a relative error of at most 0.0029.
Values may be sent and summed in bfloat16 or wider, within the bound.
No kernel may reach another device: no remote copies, remote signals or barrier semaphores. Data moves between devices by JAX's collectives and lax.ppermute only.
A program may use at most 64 MiB of HBM per device.

```python
import math
import jax
import jax.numpy as jnp
import numpy as np
from jax import lax

CX = 8
CY = 128
NZ = 256
TS = 128
TR_DEV = 32
TOP = 2
STEPS = 16
CAP = 8
NX = 64
NY = 512
SENSORS = 1024
N_SLAB = 8
N_GRP = 4


def plant(values, stream_key, low, high):
    longest = values.shape.index(max(values.shape))
    spots = []
    for shift in (0, 1):
        where = [jax.random.randint(jax.random.fold_in(stream_key, axis), (), 0, length) for axis, length in enumerate(values.shape)]
        where[longest] = (where[longest] + shift) % values.shape[longest]
        spots.append(tuple(where))
    return values.at[spots[0]].set(low).at[spots[1]].set(high)


def block_scale(stream_key, shape, split, low, largest):
    gain = 1.0
    for dim, blocks in split:
        steps = jax.random.uniform(jax.random.fold_in(jax.random.fold_in(stream_key, 6), dim), (blocks,), jnp.float32, low / len(split), largest / len(split))
        gain = gain * jnp.repeat(jnp.exp(steps), shape[dim] // blocks).reshape((-1,) + (1,) * (len(shape) - 1 - dim))
    return gain


def deal_out(key, own, number, rows, count, top, bound, slope):
    ranking = jax.random.permutation(key, count)
    crowded, common = shares(count, rows * top, bound, slope, True), shares(count, rows * top, bound, slope, False)
    places = jnp.arange(count)

    def named(tallies, offset_by):
        used = int((tallies > 0).sum())
        fixed = max(1, used // 4)
        shifted = fixed + (places - fixed + offset_by * (used - fixed)) % max(1, count - fixed)
        return jnp.zeros((count,), jnp.int32).at[ranking[jnp.where(places < fixed, places, shifted)]].set(jnp.asarray(tallies, jnp.int32))

    tallies = jnp.where(number % 4 == 0, named(crowded, number // 4), named(common, number - number // 4 - 1))
    mixed = jax.random.permutation(jax.random.fold_in(own, 3), count)
    giver, receiver = mixed[0:count // 2 * 2:2], mixed[1:count // 2 * 2:2]
    slack = jnp.minimum(tallies[giver] - 1, bound - tallies[receiver]) // 2
    slack = jnp.where((giver == ranking[0]) | (receiver == ranking[0]) | (tallies[receiver] == 0), 0, jnp.maximum(slack, 0))
    shifted = jax.random.randint(jax.random.fold_in(own, 4), (count // 2,), 0, 1 << 20) % (slack + 1)
    tallies = tallies.at[giver].add(-shifted).at[receiver].add(shifted)
    items = jnp.searchsorted(jnp.cumsum(tallies), jnp.arange(rows * top), side="right").astype(jnp.int32)
    grid = items.reshape(top, rows).T
    grid = grid[jax.random.permutation(jax.random.fold_in(own, 1), rows)]
    offset_by = jax.random.randint(jax.random.fold_in(own, 2), (rows, 1), 0, top)
    return jnp.take_along_axis(grid, (jnp.arange(top)[None, :] + offset_by) % top, axis=1)


def shares(count, total, limit, skew, full):
    weights = [(1 << 20) // math.isqrt(standing ** skew) + 1 for standing in range(1, count + 1)]
    largest = limit if full else min(limit, max(-(-total // count), total * weights[0] // sum(weights)))
    least = 1 if total - largest >= count - 1 else 0
    holding, surplus = [largest] + [least] * (count - 1), total - largest - least * (count - 1)
    while surplus > 0:
        candidates = [i for i in range(1, count) if holding[i] < largest] or [i for i in range(1, count) if holding[i] < limit]
        mass, remaining = sum([weights[i] for i in candidates]), surplus
        for i in candidates:
            extra = min(limit - holding[i], max(1, remaining * weights[i] // mass), surplus)
            holding[i] = holding[i] + extra
            surplus = surplus - extra
    return np.array(holding)


def scatter_about(own_key, extent, deviation, limit, shards=(), kind=jnp.bfloat16):
    entries = deviation * jax.random.normal(own_key, extent, jnp.float32)
    if shards:
        entries = entries * block_scale(own_key, extent, shards, -0.22, 0.18)
    return jnp.clip(entries, -limit, limit).astype(kind)


def setup_inputs(seed: int = 0) -> dict:
    arg_keys = jax.random.split(jax.random.key(seed), 9)
    pressure = scatter_about(arg_keys[0], (NX, NY, NZ), 1.0, 6.0, ((0, 8), (1, 4)), jnp.float32)
    velocity = scatter_about(arg_keys[1], (3, NX, NY, NZ), 0.5, 6.0, ((1, 8), (2, 4)), jnp.float32)
    stiffness = jnp.clip(jnp.exp(math.log(2.5) - 0.916290732 * jax.random.uniform(arg_keys[2], (NX, NY, NZ), jnp.float32) ** block_scale(arg_keys[2], (NX, NY, NZ), ((0, 8), (1, 4)), -0.2, 0.2)), 1.0, 2.5)
    buoyancy = jnp.clip(jnp.exp(math.log(1.0) - 0.6931472 * jax.random.uniform(arg_keys[3], (NX, NY, NZ), jnp.float32) ** block_scale(arg_keys[3], (NX, NY, NZ), ((0, 8), (1, 4)), -0.2, 0.2)), 0.5, 1.0)
    traces = scatter_about(arg_keys[4], (SENSORS, TS), 1.0, 6.0, ((0, 32),))
    lateral = scatter_about(arg_keys[5], (SENSORS, TOP, CX), 0.15, 1.0, ((0, 32),))
    routes_keys = jax.random.split(jax.random.fold_in(arg_keys[6], 1), SENSORS // TR_DEV)
    routes_turns = jax.random.permutation(jax.random.fold_in(arg_keys[6], 3), SENSORS // TR_DEV)
    routes = jax.vmap(lambda own, number: deal_out(jax.random.fold_in(arg_keys[6], 2), own, number, TR_DEV, N_SLAB, TOP, CAP, 2))(routes_keys, routes_turns).reshape((SENSORS, TOP))
    ycenter = plant(jax.random.randint(arg_keys[7], (SENSORS,), 0, NY), jax.random.fold_in(arg_keys[7], 1), 0, NY - 1).astype(jnp.int32)
    return {"pressure": pressure, "velocity": velocity, "stiffness": stiffness, "buoyancy": buoyancy, "traces": traces, "lateral": lateral, "routes": routes, "ycenter": ycenter}


TIME_STEP = 0.3


def band_rows(centres, rows_y):
    distance = jnp.abs(rows_y[None, :] - centres[:, None]).astype(jnp.float32)
    return jnp.maximum(0.0, 1.0 - distance / float(CY)).astype(jnp.bfloat16)


def reference(pressure, velocity, stiffness, buoyancy, traces, lateral, routes, ycenter):
    max_rows = min(SENSORS, N_SLAB * N_GRP * CAP)
    rows_y = jnp.arange(NY, dtype=jnp.int32)
    lateral_wide = lateral.astype(jnp.float32)
    traces_wide = traces.astype(jnp.float32)

    def one_slab(target):
        matches = routes == target
        lat_rows = jnp.sum(jnp.where(matches[:, :, None], lateral_wide, 0.0), axis=1)
        sort_key = jnp.where(jnp.any(matches, axis=1), 0, 1).astype(jnp.int32)
        ordering = jnp.argsort(sort_key, stable=True)[:max_rows]
        outer_terms = (lat_rows[ordering][:, :, None] * traces_wide[ordering][:, None, :]).astype(jnp.bfloat16)
        profile = band_rows(ycenter[ordering], rows_y)
        return jnp.einsum('ry,rxz->xyz', profile.astype(jnp.float32), outer_terms.astype(jnp.float32))

    injection = lax.map(one_slab, jnp.arange(N_SLAB, dtype=jnp.int32)).reshape(NX, NY, TS)
    source = jnp.pad(injection, ((0, 0), (0, 0), (NZ - TS, 0)))

    def advance(step_at, fields):
        pres_now, vel_now = fields
        zero_x = jnp.zeros_like(pres_now[:1])
        zero_y = jnp.zeros_like(pres_now[:, :1])
        zero_z = jnp.zeros_like(pres_now[:, :, :1])
        grad_x = jnp.concatenate([pres_now[1:], zero_x], 0) - pres_now
        grad_y = jnp.concatenate([pres_now[:, 1:], zero_y], 1) - pres_now
        grad_z = jnp.concatenate([pres_now[:, :, 1:], zero_z], 2) - pres_now
        vel_x = vel_now[0] - TIME_STEP * buoyancy * grad_x
        vel_y = vel_now[1] - TIME_STEP * buoyancy * grad_y
        vel_z = vel_now[2] - TIME_STEP * buoyancy * grad_z
        divergence = vel_x - jnp.concatenate([zero_x, vel_x[:-1]], 0)
        divergence = divergence + vel_y - jnp.concatenate([zero_y, vel_y[:, :-1]], 1)
        divergence = divergence + vel_z - jnp.concatenate([zero_z, vel_z[:, :, :-1]], 2)
        pres_next = pres_now - TIME_STEP * stiffness * divergence + TIME_STEP * source
        return pres_next, jnp.stack([vel_x, vel_y, vel_z])

    pres_end, vel_end = lax.fori_loop(0, STEPS, advance, (pressure, velocity))
    return pres_end, vel_end
```

```python
import functools

import jax
import jax.numpy as jnp
from jax import lax
from jax.experimental import pallas as pl
from jax.experimental.pallas import tpu as pltpu
from jax.sharding import PartitionSpec as P

TIME_STEP = 0.3
STEPS = 16
HX = 4
HY = 16
BAND = 128.0
LANES = 128
SUB = 8
CHUNK = 32
BLOCK = 2
BF16 = jnp.bfloat16
F32 = jnp.float32
VM = pl.BlockSpec(memory_space=pltpu.VMEM)
SM = pl.BlockSpec(memory_space=pltpu.SMEM)


def passed_along(value, axis, steps):
    count = lax.axis_size(axis)
    first, last = (max(0, -steps), min(count, count - steps))
    return lax.ppermute(value, axis, [(source, source + steps) for source in range(first, last)])


def params(mib):
    return pltpu.CompilerParams(vmem_limit_bytes=mib << 20)


def pack_rows_kernel(p, v, k, b, s_e, c_e, k_e, b_e, vx_e, to_ahead, to_behind):
    planes, rows, depth = p.shape

    def one_plane(x, _):
        prev = jnp.maximum(x - 1, 0)
        for r in range(0, rows, CHUNK):
            sl = pl.ds(r, CHUNK)
            dst = pl.ds(HY + r, CHUNK)
            lane = lax.broadcasted_iota(jnp.int32, (CHUNK, depth), 1)
            row = lax.broadcasted_iota(jnp.int32, (CHUNK, depth), 0)
            vx, vy, vz = v[0, x, sl, :], v[1, x, sl, :], v[2, x, sl, :]
            vx_prev = jnp.where(x > 0, v[0, prev, sl, :], 0.0)
            above = jnp.zeros((1, depth), F32) if r == 0 else v[1, x, pl.ds(r - 1, 1), :]
            vy_prev = jnp.where(row == 0, above, pltpu.roll(vy, 1, 0))
            vz_prev = jnp.where(lane == 0, 0.0, pltpu.roll(vz, 1, 1))
            div = (vx - vx_prev) + (vy - vy_prev) + (vz - vz_prev)
            kk = k[x, sl, :]
            s_e[HX + x, dst, :] = p[x, sl, :]
            c_e[HX + x, dst, :] = -TIME_STEP * kk * div
            k_e[HX + x, dst, :] = kk
            b_e[HX + x, dst, :] = b[x, sl, :]
        for i, field in enumerate((s_e, c_e, k_e, b_e)):
            to_ahead[i * planes + x] = field[HX + x, pl.ds(rows, HY), :].astype(BF16)
            to_behind[i * planes + x] = field[HX + x, pl.ds(HY, HY), :].astype(BF16)
        return 0

    lax.fori_loop(0, planes, one_plane, 0)
    vx_e[pl.ds(HY, rows), :] = v[0, planes - 1]
    to_ahead[4 * planes] = v[0, planes - 1, pl.ds(rows - HY, HY), :].astype(BF16)
    to_behind[4 * planes] = v[0, planes - 1, pl.ds(0, HY), :].astype(BF16)
    last = v[1, :, rows - 1, :]
    to_ahead[4 * planes + 1] = jnp.concatenate([last, jnp.zeros((HY - planes, depth), F32)], 0).astype(BF16)


def pack_planes_kernel(
    behind, ahead, vy_last, s_i, c_i, k_i, b_i, vx_i, s_e, c_e, k_e, b_e, vx_e, to_ahead, to_behind
):
    del s_i, c_i, k_i, b_i, vx_i
    planes = vy_last.shape[0]
    rows = s_e.shape[1] - 2 * HY
    low, high = pl.ds(0, HY), pl.ds(HY + rows, HY)
    vy_behind = behind[4 * planes + 1].astype(F32)
    for x in range(planes):
        for i, field in enumerate((s_e, c_e, k_e, b_e)):
            field[HX + x, low, :] = behind[i * planes + x].astype(F32)
            field[HX + x, high, :] = ahead[i * planes + x].astype(F32)
        first = pl.ds(HY, 1)
        c_e[HX + x, first, :] += TIME_STEP * k_e[HX + x, first, :] * vy_behind[x : x + 1]
        beyond = pl.ds(HY + rows, 1)
        c_e[HX + x, beyond, :] += TIME_STEP * k_e[HX + x, beyond, :] * vy_last[x : x + 1, :]
    vx_e[low, :] = behind[4 * planes].astype(F32)
    vx_e[high, :] = ahead[4 * planes].astype(F32)
    at = 0
    for field, skip in ((s_e, 0), (c_e, 1), (k_e, 1), (b_e, 0)):
        for x in range(planes + skip, planes + HX):
            to_ahead[at] = field[x].astype(BF16)
            at += 1
    to_ahead[at] = vx_e[...].astype(BF16)
    at = 0
    for field, skip in ((s_e, 0), (c_e, 1), (k_e, 1), (b_e, 1)):
        for x in range(HX, 2 * HX - skip):
            to_behind[at] = field[x].astype(BF16)
            at += 1


def source_kernel(where_at, centre, routes, gathered, src):
    planes, rows, samples = src.shape
    sensors = gathered.shape[0]
    own_planes = planes - 2 * HX
    slab_at, row_from, row_count = where_at[0], where_at[1], where_at[2]
    row_at = row_from + lax.broadcasted_iota(jnp.int32, (rows, sensors), 0)
    distance = jnp.abs(row_at - centre[...]).astype(F32)
    band = jnp.maximum(0.0, 1.0 - distance / BAND)
    band = jnp.where((row_at >= 0) & (row_at < row_count), band, 0.0).astype(BF16)
    column = lax.broadcasted_iota(jnp.int32, (sensors, planes), 1)
    target = slab_at + jnp.where(column < HX, -1, jnp.where(column < HX + own_planes, 0, 1))
    weights = jnp.zeros((sensors, planes), F32)
    for i in range(routes.shape[1]):
        lat = gathered[:, samples + i * planes : samples + (i + 1) * planes].astype(F32)
        weights = weights + jnp.where(routes[:, i : i + 1] == target, lat, 0.0)
    trace = gathered[:, :samples].astype(F32)
    for x in range(planes):
        outer = (weights[:, x : x + 1] * trace).astype(BF16)
        src[x] = jnp.dot(band, outer, preferred_element_type=F32)


def tile(x, t, h):
    return (x, pl.ds(SUB * t, SUB), pl.ds(LANES * h, LANES))


def advance_planes(s, o, coef, x, count, t0, t1):
    c, a, ax, ay, az, d = coef
    row = lax.broadcasted_iota(jnp.int32, (SUB, LANES), 0)
    lane = lax.broadcasted_iota(jnp.int32, (SUB, LANES), 1)
    halves = range(s.shape[2] // LANES)

    def around(t):
        here = [[s[tile(x + i, t, h)] for h in halves] for i in range(count)]
        up = [[pltpu.roll(v, SUB - 1, 0) for v in q] for q in here]
        down = [[pltpu.roll(v, 1, 0) for v in q] for q in here]
        return here, up, down

    here, up, down = around(t0)
    down_prev = down
    for t in range(t0, t1):
        later, up_next, down_next = around(t + 1) if t + 1 < t1 else (here, up, down)
        before = [s[tile(x - 1, t, h)] for h in halves]
        for i in range(count):
            now = here[i]
            after = here[i + 1] if i + 1 < count else [s[tile(x + count, t, h)] for h in halves]
            right = [pltpu.roll(v, LANES - 1, 1) for v in now] + [jnp.zeros((SUB, LANES), F32)]
            left = [pltpu.roll(v, 1, 1) for v in now]
            for h in halves:
                at = tile(x + i, t, h)
                y_next = jnp.where(row == SUB - 1, up_next[i][h], up[i][h])
                y_prev = jnp.where(row == 0, down_prev[i][h], down[i][h])
                z_next = jnp.where(lane == LANES - 1, right[h + 1], right[h])
                z_prev = left[0] if h == 0 else jnp.where(lane == 0, left[h - 1], left[h])
                moved = a[at] * (after[h] + y_next + z_next) + ax[at] * before[h]
                moved = moved + ay[at] * y_prev + az[at] * z_prev + d[at] * now[h]
                o[at] = moved + (c[at] - o[at])
            before = now
        here, up, down, down_prev = later, up_next, down_next, down


def advance_round(s, o, coef, done):
    planes, rows, _ = s.shape
    fields = [s, o]
    for step in range(1, HX + 1):
        now, then = fields[(step - 1) % 2], fields[step % 2]
        skip = (done + step - 1) // SUB
        t0, t1 = skip, rows // SUB - skip

        def some_planes(i, _, now=now, then=then, step=step, t0=t0, t1=t1):
            advance_planes(now, then, coef, step + i * BLOCK, BLOCK, t0, t1)
            return 0

        lax.fori_loop(0, (planes - 2 * step) // BLOCK, some_planes, 0)


def pack_state(s, o, to_ahead, to_behind, skip):
    planes, rows, _ = s.shape
    own = planes - 2 * HX
    sl = pl.ds(skip, rows - 2 * skip)
    for i in range(HX):
        to_ahead[i] = s[own + i, sl, :].astype(BF16)
        to_behind[i] = s[HX + i, sl, :].astype(BF16)
    for i in range(1, HX):
        to_ahead[HX + i - 1] = (s[own + i, sl, :] - o[own + i, sl, :]).astype(BF16)
        to_behind[HX + i - 1] = (s[HX + i - 1, sl, :] - o[HX + i - 1, sl, :]).astype(BF16)


def first_round_kernel(
    behind, ahead, src, k_e, b_e, vx_e, s_i, c_i, s, o, c, a, ax, ay, az, d, to_ahead, to_behind
):
    del s_i, c_i
    planes, rows, depth = s.shape
    edge = planes - HX
    at = 0
    for field, skip in ((s, 0), (c, 1), (k_e, 1), (b_e, 0)):
        for x in range(skip, HX):
            field[x] = behind[at].astype(F32)
            at += 1
    vx_behind = behind[at]
    at = 0
    for field, skip in ((s, 0), (c, 1), (k_e, 1), (b_e, 1)):
        for x in range(edge, planes - skip):
            field[x] = ahead[at].astype(F32)
            at += 1
    c[HX] += TIME_STEP * k_e[HX] * vx_behind.astype(F32)
    c[edge] += TIME_STEP * k_e[edge] * vx_e[...]
    zeros = jnp.zeros((CHUNK, depth), F32)

    def one_plane(x, _):
        for r in range(0, rows, CHUNK):
            sl = pl.ds(r, CHUNK)
            row = lax.broadcasted_iota(jnp.int32, (CHUNK, depth), 0)
            lane = lax.broadcasted_iota(jnp.int32, (CHUNK, depth), 1)
            kk = TIME_STEP * TIME_STEP * k_e[x, sl, :]
            bb = b_e[x, sl, :]
            b_x = b_e[x - 1, sl, :]
            above = b_e[x, pl.ds(max(r - 1, 0), 1), :]
            b_y = jnp.where(row == 0, above, pltpu.roll(bb, 1, 0))
            b_z = jnp.where(lane == 0, 0.0, pltpu.roll(bb, 1, 1))
            a[x, sl, :] = kk * bb
            ax[x, sl, :] = kk * b_x
            ay[x, sl, :] = kk * b_y
            az[x, sl, :] = kk * b_z
            d[x, sl, :] = 2.0 - kk * (3.0 * bb + b_x + b_y + b_z)
            c[x, sl, pl.ds(depth - src.shape[2], src.shape[2])] += TIME_STEP * src[x, sl, :]
        return 0

    lax.fori_loop(1, planes - 1, one_plane, 0)

    def clear(x, _):
        for r in range(0, rows, CHUNK):
            o[x, pl.ds(r, CHUNK), :] = zeros
        return 0

    lax.fori_loop(0, planes, clear, 0)
    advance_round(s, o, (c, a, ax, ay, az, d), 0)
    pack_state(s, o, to_ahead, to_behind, 0)


def take_halo(behind, ahead, s, o, skip):
    planes, rows, _ = s.shape
    edge = planes - HX
    sl = pl.ds(skip, rows - 2 * skip)
    for i in range(HX):
        s[i, sl, :] = behind[i].astype(F32)
        s[edge + i, sl, :] = ahead[i].astype(F32)
    for i in range(1, HX):
        o[i, sl, :] = s[i, sl, :] - behind[HX + i - 1].astype(F32)
        o[edge + i - 1, sl, :] = s[edge + i - 1, sl, :] - ahead[HX + i - 1].astype(F32)


def middle_round_kernel(behind, ahead, c, a, ax, ay, az, d, s_i, o_i, s, o, to_ahead, to_behind, *, done, skips):
    del s_i, o_i
    take_halo(behind, ahead, s, o, skips[0])
    advance_round(s, o, (c, a, ax, ay, az, d), done)
    pack_state(s, o, to_ahead, to_behind, skips[1])


def last_round_kernel(
    behind, ahead, c, a, ax, ay, az, d, b_e, v, s_i, o_i, p_out, v_out, s, o, *, done, skip
):
    del s_i, o_i
    take_halo(behind, ahead, s, o, skip)
    advance_round(s, o, (c, a, ax, ay, az, d), done)
    planes, rows, depth = p_out.shape

    def one_plane(x, _):
        for r in range(0, rows, CHUNK):
            sl, src = pl.ds(r, CHUNK), pl.ds(HY + r, CHUNK)
            row = lax.broadcasted_iota(jnp.int32, (CHUNK, depth), 0)
            lane = lax.broadcasted_iota(jnp.int32, (CHUNK, depth), 1)
            total = o[HX + x, src, :]
            p_out[x, sl, :] = s[HX + x, src, :] - total
            below = o[HX + x, pl.ds(HY + r + CHUNK, 1), :]
            y_next = jnp.where(row == CHUNK - 1, below, pltpu.roll(total, CHUNK - 1, 0))
            z_next = jnp.where(lane == depth - 1, 0.0, pltpu.roll(total, depth - 1, 1))
            bb = TIME_STEP * b_e[HX + x, src, :]
            v_out[0, x, sl, :] = v[0, x, sl, :] - bb * (o[HX + x + 1, src, :] - total)
            v_out[1, x, sl, :] = v[1, x, sl, :] - bb * (y_next - total)
            v_out[2, x, sl, :] = v[2, x, sl, :] - bb * (z_next - total)
        return 0

    lax.fori_loop(0, planes, one_plane, 0)


def local(pressure, velocity, stiffness, buoyancy, traces, lateral, routes, ycenter):
    planes, rows, depth = pressure.shape
    samples = traces.shape[1]
    wide, tall = planes + 2 * HX, rows + 2 * HY
    block = pltpu.VMEM((wide, tall, depth), F32)
    line = pltpu.VMEM((tall, depth), F32)

    lat = jnp.concatenate([lateral[:, :, planes - HX :], lateral, lateral[:, :, :HX]], 2)
    rows_sent = jnp.concatenate([traces, lat.reshape(lat.shape[0], -1)], 1)
    gathered = lax.all_gather(rows_sent, "grp", tiled=True)
    gathered = lax.all_gather(gathered, "slab", tiled=True)

    units = 4 * planes
    s, c, k_e, b_e, vx_e, row_ahead, row_behind = pl.pallas_call(
        pack_rows_kernel,
        out_shape=(
            block, block, block, block, line,
            jax.ShapeDtypeStruct((units + 2, HY, depth), BF16),
            jax.ShapeDtypeStruct((units + 1, HY, depth), BF16),
        ),
        in_specs=[VM] * 4,
        out_specs=[VM] * 7,
        compiler_params=params(16),
    )(pressure, velocity, stiffness, buoyancy)
    from_behind = passed_along(row_ahead, "grp", 1)
    from_ahead = passed_along(row_behind, "grp", -1)

    n_ahead, n_behind = 4 * HX - 1, 4 * HX - 3
    s, c, k_e, b_e, vx_e, plane_ahead, plane_behind = pl.pallas_call(
        pack_planes_kernel,
        out_shape=(
            block, block, block, block, line,
            jax.ShapeDtypeStruct((n_ahead, tall, depth), BF16),
            jax.ShapeDtypeStruct((n_behind, tall, depth), BF16),
        ),
        in_specs=[VM] * 8,
        out_specs=[VM] * 7,
        input_output_aliases={3: 0, 4: 1, 5: 2, 6: 3, 7: 4},
        compiler_params=params(16),
    )(from_behind, from_ahead, velocity[1, :, rows - 1, :], s, c, k_e, b_e, vx_e)
    from_behind = passed_along(plane_ahead, "slab", 1)
    from_ahead = passed_along(plane_behind, "slab", -1)

    where_at = jnp.stack(
        [
            lax.axis_index("slab"),
            lax.axis_index("grp") * rows - HY,
            jnp.int32(rows * lax.axis_size("grp")),
        ]
    ).astype(jnp.int32)
    src = pl.pallas_call(
        source_kernel,
        out_shape=pltpu.VMEM((wide, tall, samples), F32),
        in_specs=[SM, VM, VM, VM],
        out_specs=VM,
        compiler_params=params(16),
    )(where_at, ycenter[None, :], routes, gathered)

    def sent(skip):
        return jax.ShapeDtypeStruct((2 * HX - 1, tall - 2 * skip, depth), BF16)

    s, o, c, a, ax, ay, az, d, plane_ahead, plane_behind = pl.pallas_call(
        first_round_kernel,
        out_shape=(block,) * 8 + (sent(0), sent(0)),
        in_specs=[VM] * 8,
        out_specs=[VM] * 10,
        input_output_aliases={6: 0, 7: 2},
        compiler_params=params(16),
    )(from_behind, from_ahead, src, k_e, b_e, vx_e, s, c)
    coef = (c, a, ax, ay, az, d)

    rounds = STEPS // HX
    skips = [SUB * (HX * r // SUB) for r in range(1, rounds)]
    for r in range(1, rounds - 1):
        from_behind = passed_along(plane_ahead, "slab", 1)
        from_ahead = passed_along(plane_behind, "slab", -1)
        s, o, plane_ahead, plane_behind = pl.pallas_call(
            functools.partial(middle_round_kernel, done=HX * r, skips=skips[r - 1 : r + 1]),
            out_shape=(block, block, sent(skips[r]), sent(skips[r])),
            in_specs=[VM] * 10,
            out_specs=[VM] * 4,
            input_output_aliases={8: 0, 9: 1},
            compiler_params=params(16),
        )(from_behind, from_ahead, *coef, s, o)
    from_behind = passed_along(plane_ahead, "slab", 1)
    from_ahead = passed_along(plane_behind, "slab", -1)
    return pl.pallas_call(
        functools.partial(last_round_kernel, done=HX * (rounds - 1), skip=skips[-1]),
        out_shape=(
            jax.ShapeDtypeStruct(pressure.shape, F32),
            jax.ShapeDtypeStruct(velocity.shape, F32),
            block,
            block,
        ),
        in_specs=[VM] * 12,
        out_specs=[VM] * 4,
        input_output_aliases={10: 2, 11: 3},
        compiler_params=params(16),
    )(from_behind, from_ahead, *coef, b_e, velocity, s, o)[:2]


def solution(mesh):
    in_specs = (
        P("slab", "grp", None),
        P(None, "slab", "grp", None),
        P("slab", "grp", None),
        P("slab", "grp", None),
        P(("slab", "grp"), None),
        P(("slab", "grp"), None, None),
        P(),
        P(),
    )
    out_specs = (P("slab", "grp", None), P(None, "slab", "grp", None))
    return jax.shard_map(local, mesh=mesh, in_specs=in_specs, out_specs=out_specs, check_vma=False)
```

```python
import functools

import jax
import jax.numpy as jnp
from jax import lax
from jax.experimental import pallas as pl
from jax.experimental.pallas import tpu as pltpu
from jax.sharding import PartitionSpec as P

TIME_STEP = 0.3
STEPS = 16
HX = 4
HY = 16
BAND = 128.0
LANES = 128
SUB = 8
CHUNK = 32
BLOCK = 2
S, C, K, B, O, A, AX, AY, AZ, D = range(10)
FIELDS = 10
BF16 = jnp.bfloat16
F32 = jnp.float32
VM = pl.BlockSpec(memory_space=pltpu.VMEM)
HBM = pl.BlockSpec(memory_space=pltpu.HBM)


def passed_along(value, axis, steps):
    count = lax.axis_size(axis)
    first, last = (max(0, -steps), min(count, count - steps))
    return lax.ppermute(value, axis, [(source, source + steps) for source in range(first, last)])


def params(mib):
    return pltpu.CompilerParams(vmem_limit_bytes=mib << 20)


def main_planes(planes):
    ahead = [(f, planes + skip, HX - skip) for f, skip in enumerate((0, 1, 1, 0))]
    behind = [(f, HX, HX - skip) for f, skip in enumerate((0, 1, 1, 1))]
    return ahead, behind


def unit_list(spans):
    return [(f, x) for f, first, count in spans for x in range(first, first + count)]


def pack_kernel(p, v, k, b, c, row_ahead, row_behind, plane_ahead, plane_behind, held, sems):
    planes, rows, depth = p.shape
    p_e, k_e, b_e = (held.at[i] for i in range(3, 6))

    def copies(x):
        pairs = [(v.at[i, x], held.at[i, x]) for i in range(3)]
        pairs = pairs + [(src.at[x], dst.at[x]) for src, dst in ((k, k_e), (p, p_e), (b, b_e))]
        return [pltpu.make_async_copy(src, dst, sems.at[i, x]) for i, (src, dst) in enumerate(pairs)]

    def start(x, _):
        for copy in copies(x):
            copy.start()
        return 0

    lax.fori_loop(0, planes, start, 0)
    fields = (p_e, c, k_e, b_e)

    def one_plane(x, _):
        for copy in copies(x):
            copy.wait()
        prev = jnp.maximum(x - 1, 0)
        for r in range(0, rows, CHUNK):
            sl = pl.ds(r, CHUNK)
            lane = lax.broadcasted_iota(jnp.int32, (CHUNK, depth), 1)
            row = lax.broadcasted_iota(jnp.int32, (CHUNK, depth), 0)
            vx, vy, vz = held[0, x, sl, :], held[1, x, sl, :], held[2, x, sl, :]
            vx_prev = jnp.where(x > 0, held[0, prev, sl, :], 0.0)
            above = jnp.zeros((1, depth), F32) if r == 0 else held[1, x, pl.ds(r - 1, 1), :]
            vy_prev = jnp.where(row == 0, above, pltpu.roll(vy, 1, 0))
            vz_prev = jnp.where(lane == 0, 0.0, pltpu.roll(vz, 1, 1))
            div = (vx - vx_prev) + (vy - vy_prev) + (vz - vz_prev)
            c[x, sl, :] = -TIME_STEP * k_e[x, sl, :] * div
        for f, field in enumerate(fields):
            row_ahead[f * planes + x] = field[x, pl.ds(rows - HY, HY), :].astype(BF16)
            row_behind[f * planes + x] = field[x, pl.ds(0, HY), :].astype(BF16)
        return 0

    lax.fori_loop(0, planes, one_plane, 0)
    ahead, behind = main_planes(planes)
    for out, spans in ((plane_ahead, ahead), (plane_behind, behind)):
        for i, (f, x) in enumerate(unit_list(spans)):
            out[i] = fields[f][x - HX].astype(BF16)
    plane_ahead[len(unit_list(ahead))] = held[0, planes - 1].astype(BF16)
    row_ahead[4 * planes] = held[0, planes - 1, pl.ds(rows - HY, HY), :].astype(BF16)
    row_behind[4 * planes] = held[0, planes - 1, pl.ds(0, HY), :].astype(BF16)
    edge = held[1, :, rows - 1, :]
    row_ahead[4 * planes + 1] = jnp.concatenate([edge, jnp.zeros((HY - planes, depth), F32)], 0).astype(BF16)


def corner_kernel(behind, ahead, own_ahead, own_behind, to_ahead, to_behind):
    planes = (behind.shape[0] - 2) // 4
    depth = behind.shape[2]
    row = lax.broadcasted_iota(jnp.int32, (HY, depth), 0)
    vy_behind = behind[4 * planes + 1].astype(F32)
    vy_last = own_ahead[4 * planes + 1].astype(F32)
    for out, spans in zip((to_ahead, to_behind), main_planes(planes)):
        units = unit_list(spans)
        deltas = []
        for i, (f, x) in enumerate(units):
            x = x - HX
            out[2 * i] = behind[f * planes + x]
            got = ahead[f * planes + x]
            if f == C:
                got = got.astype(F32)
                fix = TIME_STEP * ahead[K * planes + x].astype(F32) * vy_last[x : x + 1]
                got = jnp.where(row == 0, got + fix, got).astype(BF16)
                near = own_behind[K * planes + x].astype(F32)[:1]
                deltas.append(TIME_STEP * near * vy_behind[x : x + 1])
            out[2 * i + 1] = got
        deltas = jnp.concatenate(deltas + [jnp.zeros((HY - len(deltas), depth), F32)], 0)
        out[2 * len(units)] = deltas.astype(BF16)
    at = len(unit_list(main_planes(planes)[0]))
    to_ahead[2 * at + 1] = behind[4 * planes]
    to_ahead[2 * at + 2] = ahead[4 * planes]


def repeat_kernel(got, copies):
    for i in range(copies.shape[0]):
        copies[i] = got[...].reshape(copies.shape[1:])


def source_kernel(centre, routes, gathered, src, *, held):
    planes, rows, samples = src.shape
    groups, sensors, _ = gathered.shape
    slabs = sensors // held
    sensors = sensors * groups
    own_rows = rows - 2 * HY
    row_at = lax.axis_index("grp") * own_rows - HY + lax.broadcasted_iota(jnp.int32, (rows, sensors), 0)
    distance = jnp.abs(row_at - centre[...]).astype(F32)
    band = jnp.maximum(0.0, 1.0 - distance / BAND)
    band = jnp.where((row_at >= 0) & (row_at < own_rows * groups), band, 0.0).astype(BF16)
    parts = [gathered[g, pl.ds(held * t, held), :] for t in range(slabs) for g in range(groups)]
    ordered = jnp.concatenate(parts, 0)
    column = lax.broadcasted_iota(jnp.int32, (sensors, planes), 1)
    target = jnp.where(column < HX, -1, jnp.where(column < planes - HX, 0, 1)) + lax.axis_index("slab")
    weights = jnp.zeros((sensors, planes), F32)
    for i in range(routes.shape[1]):
        lat = ordered[:, samples + i * planes : samples + (i + 1) * planes].astype(F32)
        weights = weights + jnp.where(routes[:, i : i + 1] == target, lat, 0.0)
    trace = ordered[:, :samples].astype(F32)
    for x in range(1, planes - 1):
        outer = (weights[:, x : x + 1] * trace).astype(BF16)
        src[x] = TIME_STEP * jnp.dot(band, outer, preferred_element_type=F32)


def tile(x, t, h):
    return (x, pl.ds(SUB * t, SUB), pl.ds(LANES * h, LANES))


def advance_planes(s, o, coef, x, count, t0, t1):
    c, a, ax, ay, az, d = coef
    row = lax.broadcasted_iota(jnp.int32, (SUB, LANES), 0)
    lane = lax.broadcasted_iota(jnp.int32, (SUB, LANES), 1)
    halves = range(s.shape[2] // LANES)

    def around(t):
        here = [[s[tile(x + i, t, h)] for h in halves] for i in range(count)]
        up = [[pltpu.roll(v, SUB - 1, 0) for v in q] for q in here]
        down = [[pltpu.roll(v, 1, 0) for v in q] for q in here]
        return here, up, down

    here, up, down = around(t0)
    down_prev = down
    for t in range(t0, t1):
        later, up_next, down_next = around(t + 1) if t + 1 < t1 else (here, up, down)
        before = [s[tile(x - 1, t, h)] for h in halves]
        for i in range(count):
            now = here[i]
            after = here[i + 1] if i + 1 < count else [s[tile(x + count, t, h)] for h in halves]
            right = [pltpu.roll(v, LANES - 1, 1) for v in now] + [jnp.zeros((SUB, LANES), F32)]
            left = [pltpu.roll(v, 1, 1) for v in now]
            for h in halves:
                at = tile(x + i, t, h)
                y_next = jnp.where(row == SUB - 1, up_next[i][h], up[i][h])
                y_prev = jnp.where(row == 0, down_prev[i][h], down[i][h])
                z_next = jnp.where(lane == LANES - 1, right[h + 1], right[h])
                z_prev = left[0] if h == 0 else jnp.where(lane == 0, left[h - 1], left[h])
                moved = a[at] * (after[h] + y_next + z_next) + ax[at] * before[h]
                moved = moved + ay[at] * y_prev + az[at] * z_prev + d[at] * now[h]
                o[at] = moved + (c[at] - o[at])
            before = now
        here, up, down, down_prev = later, up_next, down_next, down


def advance_round(store, done):
    planes, rows = store.shape[1:3]
    fields = [store.at[S], store.at[O]]
    coef = [store.at[f] for f in (C, A, AX, AY, AZ, D)]
    for step in range(1, HX + 1):
        now, then = fields[(step - 1) % 2], fields[step % 2]
        skip = (done + step - 1) // SUB
        t0, t1 = skip, rows // SUB - skip

        def some_planes(i, _, now=now, then=then, step=step, t0=t0, t1=t1):
            advance_planes(now, then, coef, step + i * BLOCK, BLOCK, t0, t1)
            return 0

        lax.fori_loop(0, (planes - 2 * step) // BLOCK, some_planes, 0)


def pack_state(store, to_ahead, to_behind, skip):
    planes, rows = store.shape[1:3]
    own = planes - 2 * HX
    sl = pl.ds(skip, rows - 2 * skip)
    for i in range(HX):
        to_ahead[i] = store[S, own + i, sl, :].astype(BF16)
        to_behind[i] = store[S, HX + i, sl, :].astype(BF16)
    for i in range(1, HX):
        for out, x in ((to_ahead, own + i), (to_behind, HX + i - 1)):
            out[HX + i - 1] = (store[S, x, sl, :] - store[O, x, sl, :]).astype(BF16)


def first_round_kernel(*refs):
    given, (p, v, k, b, c, store, to_ahead, to_behind) = refs[:8], refs[8:16]
    taken, (line, sems) = refs[16:24], refs[24:]
    behind, ahead, corner_behind, corner_ahead, row_behind, row_ahead, own_ahead, src = taken
    takes = [pltpu.make_async_copy(given[i], taken[i], sems.at[5 + i]) for i in range(8)]
    planes, rows, depth = store.shape[1:]
    edge = planes - HX
    own_rows = rows - 2 * HY
    own = planes - 2 * HX
    low, middle, high = pl.ds(0, HY), pl.ds(HY, own_rows), pl.ds(HY + own_rows, HY)
    inner = pl.ds(HX, own)
    copies = [
        pltpu.make_async_copy(part, store.at[f, inner, middle, :], sems.at[f])
        for f, part in ((S, p), (C, c), (K, k), (B, b))
    ]
    copies.append(pltpu.make_async_copy(v.at[0, own - 1], line.at[middle, :], sems.at[4]))
    for copy in takes + copies:
        copy.start()
    for copy in takes:
        copy.wait()
    sent_ahead, sent_behind = main_planes(own)
    moves = ((behind, corner_behind, sent_ahead, -own), (ahead, corner_ahead, sent_behind, own))
    for main, corner, spans, shift in moves:
        units = unit_list(spans)
        for i, (f, x) in enumerate(units):
            store[f, x + shift, low, :] = corner[2 * i].astype(F32)
            store[f, x + shift, middle, :] = main[i].astype(F32)
            store[f, x + shift, high, :] = corner[2 * i + 1].astype(F32)
        _, x, count = spans[1]
        fixed = corner[2 * len(units)].astype(F32)
        for i in range(count):
            store[C, x + shift + i, pl.ds(HY, 1), :] += fixed[i : i + 1]
    for x in range(own):
        for f in (S, C, K, B):
            store[f, HX + x, low, :] = row_behind[f * own + x].astype(F32)
            store[f, HX + x, high, :] = row_ahead[f * own + x].astype(F32)
    line[low, :] = row_behind[4 * own].astype(F32)
    line[high, :] = row_ahead[4 * own].astype(F32)
    vy_behind = row_behind[4 * own + 1].astype(F32)
    vy_last = own_ahead[4 * own + 1].astype(F32)
    for copy in copies:
        copy.wait()
    for x in range(own):
        for at, vy in ((HY, vy_behind), (HY + own_rows, vy_last)):
            sl = pl.ds(at, 1)
            store[C, HX + x, sl, :] += TIME_STEP * store[K, HX + x, sl, :] * vy[x : x + 1]
    at = len(unit_list(sent_ahead))
    vx_parts = ((low, corner_behind[2 * at + 1]), (middle, behind[at]), (high, corner_behind[2 * at + 2]))
    for sl, part in vx_parts:
        store[C, HX, sl, :] += TIME_STEP * store[K, HX, sl, :] * part.astype(F32)
        store[C, edge, sl, :] += TIME_STEP * store[K, edge, sl, :] * line[sl, :]
    later = pl.ds(depth - src.shape[2], src.shape[2])

    def one_plane(x, _):
        for r in range(0, rows, CHUNK):
            sl = pl.ds(r, CHUNK)
            row = lax.broadcasted_iota(jnp.int32, (CHUNK, depth), 0)
            lane = lax.broadcasted_iota(jnp.int32, (CHUNK, depth), 1)
            kk = TIME_STEP * TIME_STEP * store[K, x, sl, :]
            bb = store[B, x, sl, :]
            b_x = store[B, x - 1, sl, :]
            above = store[B, x, pl.ds(max(r - 1, 0), 1), :]
            b_y = jnp.where(row == 0, above, pltpu.roll(bb, 1, 0))
            b_z = jnp.where(lane == 0, 0.0, pltpu.roll(bb, 1, 1))
            store[A, x, sl, :] = kk * bb
            store[AX, x, sl, :] = kk * b_x
            store[AY, x, sl, :] = kk * b_y
            store[AZ, x, sl, :] = kk * b_z
            store[D, x, sl, :] = 2.0 - kk * (3.0 * bb + b_x + b_y + b_z)
            store[O, x, sl, :] = jnp.zeros((CHUNK, depth), F32)
            store[C, x, sl, later] += src[x, sl, :]
        return 0

    lax.fori_loop(1, planes - 1, one_plane, 0)
    advance_round(store, 0)
    pack_state(store, to_ahead, to_behind, 0)


def take_halo(behind, ahead, store, skip):
    planes, rows = store.shape[1:3]
    edge = planes - HX
    sl = pl.ds(skip, rows - 2 * skip)
    for i in range(HX):
        store[S, i, sl, :] = behind[i].astype(F32)
        store[S, edge + i, sl, :] = ahead[i].astype(F32)
    for i in range(1, HX):
        for x, got in ((i, behind), (edge + i - 1, ahead)):
            store[O, x, sl, :] = store[S, x, sl, :] - got[HX + i - 1].astype(F32)


def middle_round_kernel(behind, ahead, store_i, store, to_ahead, to_behind, *, done, skips):
    del store_i
    take_halo(behind, ahead, store, skips[0])
    advance_round(store, done)
    pack_state(store, to_ahead, to_behind, skips[1])


def last_round_kernel(behind, ahead, v, store_i, p_out, v_out, store, held, in_sems, out_sems, *, done, skip):
    del store_i
    planes, rows, depth = p_out.shape
    own = pl.ds(HY, rows)

    def reads(x):
        return [pltpu.make_async_copy(v.at[i, x], held.at[i, x], in_sems.at[i, x]) for i in range(3)]

    def writes(x):
        pairs = [(f, v_out.at[i, x]) for i, f in enumerate((A, AX, AY))] + [(AZ, p_out.at[x])]
        return [
            pltpu.make_async_copy(store.at[f, HX + x, own, :], dst, out_sems.at[i, x])
            for i, (f, dst) in enumerate(pairs)
        ]

    def start(x, _):
        for copy in reads(x):
            copy.start()
        return 0

    lax.fori_loop(0, planes, start, 0)
    take_halo(behind, ahead, store, skip)
    advance_round(store, done)

    def one_plane(x, _):
        for copy in reads(x):
            copy.wait()
        for r in range(0, rows, CHUNK):
            sl, at = pl.ds(r, CHUNK), pl.ds(HY + r, CHUNK)
            row = lax.broadcasted_iota(jnp.int32, (CHUNK, depth), 0)
            lane = lax.broadcasted_iota(jnp.int32, (CHUNK, depth), 1)
            total = store[O, HX + x, at, :]
            below = store[O, HX + x, pl.ds(HY + r + CHUNK, 1), :]
            y_next = jnp.where(row == CHUNK - 1, below, pltpu.roll(total, CHUNK - 1, 0))
            z_next = jnp.where(lane == depth - 1, 0.0, pltpu.roll(total, depth - 1, 1))
            bb = TIME_STEP * store[B, HX + x, at, :]
            store[A, HX + x, at, :] = held[0, x, sl, :] - bb * (store[O, HX + x + 1, at, :] - total)
            store[AX, HX + x, at, :] = held[1, x, sl, :] - bb * (y_next - total)
            store[AY, HX + x, at, :] = held[2, x, sl, :] - bb * (z_next - total)
            store[AZ, HX + x, at, :] = store[S, HX + x, at, :] - total
        for copy in writes(x):
            copy.start()
        return 0

    lax.fori_loop(0, planes, one_plane, 0)

    def finish(x, _):
        for copy in writes(x):
            copy.wait()
        return 0

    lax.fori_loop(0, planes, finish, 0)


def local(pressure, velocity, stiffness, buoyancy, traces, lateral, routes, ycenter):
    planes, rows, depth = pressure.shape
    wide, tall = planes + 2 * HX, rows + 2 * HY
    store_shape = pltpu.VMEM((FIELDS, wide, tall, depth), F32)
    slabs, groups = lax.axis_size("slab"), lax.axis_size("grp")

    def sent(count, height):
        return jax.ShapeDtypeStruct((count, height, depth), BF16)

    def everyones(copies, axis):
        return lax.all_to_all(copies, axis, split_axis=0, concat_axis=0, tiled=True)

    lat = jnp.concatenate([lateral[:, :, planes - HX :], lateral, lateral[:, :, :HX]], 2)
    sensor_rows = jnp.concatenate([traces, lat.reshape(lat.shape[0], -1)], 1)
    copies = jnp.broadcast_to(sensor_rows[None], (slabs,) + sensor_rows.shape)
    copies, centre, routes, pressure = lax.optimization_barrier((copies, ycenter[None, :], routes, pressure))
    got = everyones(copies, "slab")

    n_rows = 4 * planes
    n_ahead, n_behind = [len(unit_list(spans)) for spans in main_planes(planes)]
    inputs = [pltpu.with_memory_space_constraint(x, pltpu.HBM) for x in (pressure, velocity, stiffness, buoyancy)]
    c, row_ahead, row_behind, plane_ahead, plane_behind = pl.pallas_call(
        pack_kernel,
        out_shape=(
            jax.ShapeDtypeStruct(pressure.shape, F32), sent(n_rows + 2, HY), sent(n_rows + 1, HY),
            sent(n_ahead + 1, rows), sent(n_behind, rows),
        ),
        in_specs=[HBM] * 4,
        out_specs=[VM] * 5,
        scratch_shapes=[pltpu.VMEM((6,) + pressure.shape, F32), pltpu.SemaphoreType.DMA((6, planes))],
        compiler_params=params(24),
    )(*inputs)
    main_behind = passed_along(plane_ahead, "slab", 1)
    main_ahead = passed_along(plane_behind, "slab", -1)
    from_behind = passed_along(row_ahead, "grp", 1)
    from_ahead = passed_along(row_behind, "grp", -1)

    copies = pl.pallas_call(
        repeat_kernel,
        out_shape=jax.ShapeDtypeStruct((groups, slabs * sensor_rows.shape[0], sensor_rows.shape[1]), BF16),
        in_specs=[VM],
        out_specs=VM,
        compiler_params=params(4),
    )(got)
    gathered = everyones(copies, "grp")

    corner_ahead, corner_behind = pl.pallas_call(
        corner_kernel,
        out_shape=(sent(2 * n_ahead + 3, HY), sent(2 * n_behind + 1, HY)),
        in_specs=[VM] * 4,
        out_specs=[VM] * 2,
        compiler_params=params(8),
    )(from_behind, from_ahead, row_ahead, row_behind)
    corner_from_behind = passed_along(corner_ahead, "slab", 1)
    corner_from_ahead = passed_along(corner_behind, "slab", -1)

    src = pl.pallas_call(
        functools.partial(source_kernel, held=traces.shape[0]),
        out_shape=jax.ShapeDtypeStruct((wide, tall, traces.shape[1]), F32),
        in_specs=[VM] * 3,
        out_specs=VM,
        compiler_params=params(16),
    )(centre, routes, gathered)

    given = (main_behind, main_ahead, corner_from_behind, corner_from_ahead, from_behind, from_ahead, row_ahead, src)
    store, plane_ahead, plane_behind = pl.pallas_call(
        first_round_kernel,
        out_shape=(store_shape, sent(2 * HX - 1, tall), sent(2 * HX - 1, tall)),
        in_specs=[HBM] * 13,
        out_specs=[VM] * 3,
        scratch_shapes=[pltpu.VMEM(x.shape, x.dtype) for x in given]
        + [pltpu.VMEM((tall, depth), F32), pltpu.SemaphoreType.DMA((5 + len(given),))],
        compiler_params=params(14),
    )(*[pltpu.with_memory_space_constraint(x, pltpu.HBM) for x in given + (*inputs, c)])

    rounds = STEPS // HX
    skips = [SUB * (HX * r // SUB) for r in range(1, rounds)]
    for r in range(1, rounds - 1):
        from_behind = passed_along(plane_ahead, "slab", 1)
        from_ahead = passed_along(plane_behind, "slab", -1)
        height = tall - 2 * skips[r]
        store, plane_ahead, plane_behind = pl.pallas_call(
            functools.partial(middle_round_kernel, done=HX * r, skips=skips[r - 1 : r + 1]),
            out_shape=(store_shape, sent(2 * HX - 1, height), sent(2 * HX - 1, height)),
            in_specs=[VM] * 3,
            out_specs=[VM] * 3,
            input_output_aliases={2: 0},
            compiler_params=params(14),
        )(from_behind, from_ahead, store)
    from_behind = passed_along(plane_ahead, "slab", 1)
    from_ahead = passed_along(plane_behind, "slab", -1)
    p_out, v_out, _ = pl.pallas_call(
        functools.partial(last_round_kernel, done=HX * (rounds - 1), skip=skips[-1]),
        out_shape=(
            jax.ShapeDtypeStruct(pressure.shape, F32),
            jax.ShapeDtypeStruct(velocity.shape, F32),
            store_shape,
        ),
        in_specs=[VM, VM, HBM, VM],
        out_specs=[HBM, HBM, VM],
        input_output_aliases={3: 2},
        scratch_shapes=[
            pltpu.VMEM(velocity.shape, F32),
            pltpu.SemaphoreType.DMA((3, planes)),
            pltpu.SemaphoreType.DMA((4, planes)),
        ],
        compiler_params=params(14),
    )(from_behind, from_ahead, inputs[1], store)
    return p_out, v_out


def solution(mesh):
    in_specs = (
        P("slab", "grp", None),
        P(None, "slab", "grp", None),
        P("slab", "grp", None),
        P("slab", "grp", None),
        P(("slab", "grp"), None),
        P(("slab", "grp"), None, None),
        P(),
        P(),
    )
    out_specs = (P("slab", "grp", None), P(None, "slab", "grp", None))
    return jax.shard_map(local, mesh=mesh, in_specs=in_specs, out_specs=out_specs, check_vma=False)
```

```python
import functools

import jax
import jax.numpy as jnp
from jax import lax
from jax.experimental import pallas as pl
from jax.experimental.pallas import tpu as pltpu
from jax.sharding import PartitionSpec as P

TIME_STEP = 0.3
STEPS = 16
HX = 4
HY = 16
BAND = 128.0
LANES = 128
SUB = 8
CHUNK = 32
BLOCK = 2
S, C, K, B, O, A, AX, AY, AZ, D = range(10)
FIELDS = 10
BF16 = jnp.bfloat16
F32 = jnp.float32
VM = pl.BlockSpec(memory_space=pltpu.VMEM)
HBM = pl.BlockSpec(memory_space=pltpu.HBM)


def passed_along(value, axis, steps):
    count = lax.axis_size(axis)
    first, last = (max(0, -steps), min(count, count - steps))
    return lax.ppermute(value, axis, [(source, source + steps) for source in range(first, last)])


def params(mib):
    return pltpu.CompilerParams(vmem_limit_bytes=mib << 20)


def main_planes(planes):
    ahead = [(f, planes + skip, HX - skip) for f, skip in enumerate((0, 1, 1, 0))]
    behind = [(f, HX, HX - skip) for f, skip in enumerate((0, 1, 1, 1))]
    return ahead, behind


def unit_list(spans):
    return [(f, x) for f, first, count in spans for x in range(first, first + count)]


def pack_kernel(p, v, k, b, c, row_ahead, row_behind, plane_ahead, plane_behind, held, sems):
    planes, rows, depth = p.shape
    p_e, k_e, b_e = (held.at[i] for i in range(3, 6))

    def copies(x):
        pairs = [(v.at[i, x], held.at[i, x]) for i in range(3)]
        pairs = pairs + [(src.at[x], dst.at[x]) for src, dst in ((k, k_e), (p, p_e), (b, b_e))]
        return [pltpu.make_async_copy(src, dst, sems.at[i, x]) for i, (src, dst) in enumerate(pairs)]

    def start(x, _):
        for copy in copies(x):
            copy.start()
        return 0

    lax.fori_loop(0, planes, start, 0)
    fields = (p_e, c, k_e, b_e)

    def one_plane(x, _):
        for copy in copies(x):
            copy.wait()
        prev = jnp.maximum(x - 1, 0)
        for r in range(0, rows, CHUNK):
            sl = pl.ds(r, CHUNK)
            lane = lax.broadcasted_iota(jnp.int32, (CHUNK, depth), 1)
            row = lax.broadcasted_iota(jnp.int32, (CHUNK, depth), 0)
            vx, vy, vz = held[0, x, sl, :], held[1, x, sl, :], held[2, x, sl, :]
            vx_prev = jnp.where(x > 0, held[0, prev, sl, :], 0.0)
            above = jnp.zeros((1, depth), F32) if r == 0 else held[1, x, pl.ds(r - 1, 1), :]
            vy_prev = jnp.where(row == 0, above, pltpu.roll(vy, 1, 0))
            vz_prev = jnp.where(lane == 0, 0.0, pltpu.roll(vz, 1, 1))
            div = (vx - vx_prev) + (vy - vy_prev) + (vz - vz_prev)
            c[x, sl, :] = -TIME_STEP * k_e[x, sl, :] * div
        for f, field in enumerate(fields):
            row_ahead[f * planes + x] = field[x, pl.ds(rows - HY, HY), :].astype(BF16)
            row_behind[f * planes + x] = field[x, pl.ds(0, HY), :].astype(BF16)
        return 0

    lax.fori_loop(0, planes, one_plane, 0)
    ahead, behind = main_planes(planes)
    for out, spans in ((plane_ahead, ahead), (plane_behind, behind)):
        for i, (f, x) in enumerate(unit_list(spans)):
            out[i] = fields[f][x - HX].astype(BF16)
    plane_ahead[len(unit_list(ahead))] = held[0, planes - 1].astype(BF16)
    row_ahead[4 * planes] = held[0, planes - 1, pl.ds(rows - HY, HY), :].astype(BF16)
    row_behind[4 * planes] = held[0, planes - 1, pl.ds(0, HY), :].astype(BF16)
    edge = held[1, :, rows - 1, :]
    row_ahead[4 * planes + 1] = jnp.concatenate([edge, jnp.zeros((HY - planes, depth), F32)], 0).astype(BF16)


def corner_kernel(behind, ahead, own_ahead, own_behind, to_ahead, to_behind):
    planes = (behind.shape[0] - 2) // 4
    depth = behind.shape[2]
    row = lax.broadcasted_iota(jnp.int32, (HY, depth), 0)
    vy_behind = behind[4 * planes + 1].astype(F32)
    vy_last = own_ahead[4 * planes + 1].astype(F32)
    for out, spans in zip((to_ahead, to_behind), main_planes(planes)):
        units = unit_list(spans)
        deltas = []
        for i, (f, x) in enumerate(units):
            x = x - HX
            out[2 * i] = behind[f * planes + x]
            got = ahead[f * planes + x]
            if f == C:
                got = got.astype(F32)
                fix = TIME_STEP * ahead[K * planes + x].astype(F32) * vy_last[x : x + 1]
                got = jnp.where(row == 0, got + fix, got).astype(BF16)
                near = own_behind[K * planes + x].astype(F32)[:1]
                deltas.append(TIME_STEP * near * vy_behind[x : x + 1])
            out[2 * i + 1] = got
        deltas = jnp.concatenate(deltas + [jnp.zeros((HY - len(deltas), depth), F32)], 0)
        out[2 * len(units)] = deltas.astype(BF16)
    at = len(unit_list(main_planes(planes)[0]))
    to_ahead[2 * at + 1] = behind[4 * planes]
    to_ahead[2 * at + 2] = ahead[4 * planes]


def sensors_kernel(traces, lateral, copies):
    own = traces.shape[0]
    for i in range(copies.shape[0]):
        copies[i, pl.ds(0, own), :] = traces[...]
        copies[i, pl.ds(own, lateral.shape[0]), :] = jnp.zeros((lateral.shape[0], copies.shape[2]), BF16)
        copies[i, pl.ds(own, lateral.shape[0]), pl.ds(0, own)] = lateral[...]


def repeat_kernel(got, copies, *, own):
    slabs, height, samples = got.shape
    rows = got[:, :own, :].astype(F32).reshape(slabs * own, samples)
    traces = jnp.transpose(rows).astype(BF16)
    per = LANES // own
    weights = []
    for first in range(0, slabs, per):
        part = jnp.zeros((height - own, samples), F32)
        for i in range(per):
            piece = got[first + i, pl.ds(own, height - own), :].astype(F32)
            part = part + (pltpu.roll(piece, own * i, 1) if i else piece)
        weights.append(part)
    weights = jnp.concatenate(weights, 1).astype(BF16)
    for g in range(copies.shape[0]):
        copies[g, pl.ds(0, samples), :] = traces
        copies[g, pl.ds(samples, height - own), :] = weights


def tile(x, t, h):
    return (x, pl.ds(SUB * t, SUB), pl.ds(LANES * h, LANES))


def advance_planes(s, o, coef, x, count, t0, t1):
    c, a, ax, ay, az, d = coef
    row = lax.broadcasted_iota(jnp.int32, (SUB, LANES), 0)
    lane = lax.broadcasted_iota(jnp.int32, (SUB, LANES), 1)
    halves = range(s.shape[2] // LANES)

    def around(t):
        here = [[s[tile(x + i, t, h)] for h in halves] for i in range(count)]
        up = [[pltpu.roll(v, SUB - 1, 0) for v in q] for q in here]
        down = [[pltpu.roll(v, 1, 0) for v in q] for q in here]
        return here, up, down

    here, up, down = around(t0)
    down_prev = down
    for t in range(t0, t1):
        later, up_next, down_next = around(t + 1) if t + 1 < t1 else (here, up, down)
        before = [s[tile(x - 1, t, h)] for h in halves]
        for i in range(count):
            now = here[i]
            after = here[i + 1] if i + 1 < count else [s[tile(x + count, t, h)] for h in halves]
            right = [pltpu.roll(v, LANES - 1, 1) for v in now] + [jnp.zeros((SUB, LANES), F32)]
            left = [pltpu.roll(v, 1, 1) for v in now]
            for h in halves:
                at = tile(x + i, t, h)
                y_next = jnp.where(row == SUB - 1, up_next[i][h], up[i][h])
                y_prev = jnp.where(row == 0, down_prev[i][h], down[i][h])
                z_next = jnp.where(lane == LANES - 1, right[h + 1], right[h])
                z_prev = left[0] if h == 0 else jnp.where(lane == 0, left[h - 1], left[h])
                moved = a[at] * (after[h] + y_next + z_next) + ax[at] * before[h]
                moved = moved + ay[at] * y_prev + az[at] * z_prev + d[at] * now[h]
                o[at] = moved + (c[at] - o[at])
            before = now
        here, up, down, down_prev = later, up_next, down_next, down


def advance_some(store, done, inner):
    planes, rows = store.shape[1:3]
    fields = [store.at[S], store.at[O]]
    coef = [store.at[f] for f in (C, A, AX, AY, AZ, D)]
    edge = planes - HX
    for step in range(1, HX + 1):
        now, then = fields[(step - 1) % 2], fields[step % 2]
        skip = (done + step - 1) // SUB
        t0, t1 = skip, rows // SUB - skip
        if inner:
            first, count, stride, block = HX + step, (planes - 2 * HX - 2 * step) // 2, 2, 2
        else:
            first, count, stride, block = step, 2, edge - 2 * step, HX

        def some_planes(i, _, now=now, then=then, first=first, stride=stride, block=block, t0=t0, t1=t1):
            advance_planes(now, then, coef, first + i * stride, block, t0, t1)
            return 0

        if count > 0:
            lax.fori_loop(0, count, some_planes, 0)


def pack_state(store, to_ahead, to_behind, skip):
    planes, rows = store.shape[1:3]
    own = planes - 2 * HX
    sl = pl.ds(skip, rows - 2 * skip)
    for i in range(HX):
        to_ahead[i] = store[S, own + i, sl, :].astype(BF16)
        to_behind[i] = store[S, HX + i, sl, :].astype(BF16)
    for i in range(1, HX):
        for out, x in ((to_ahead, own + i), (to_behind, HX + i - 1)):
            out[HX + i - 1] = (store[S, x, sl, :] - store[O, x, sl, :]).astype(BF16)


def set_coefficients(store, x):
    rows, depth = store.shape[2:]
    for r in range(0, rows, CHUNK):
        sl = pl.ds(r, CHUNK)
        row = lax.broadcasted_iota(jnp.int32, (CHUNK, depth), 0)
        lane = lax.broadcasted_iota(jnp.int32, (CHUNK, depth), 1)
        kk = TIME_STEP * TIME_STEP * store[K, x, sl, :]
        bb = store[B, x, sl, :]
        b_x = store[B, x - 1, sl, :]
        above = store[B, x, pl.ds(max(r - 1, 0), 1), :]
        b_y = jnp.where(row == 0, above, pltpu.roll(bb, 1, 0))
        b_z = jnp.where(lane == 0, 0.0, pltpu.roll(bb, 1, 1))
        store[A, x, sl, :] = kk * bb
        store[AX, x, sl, :] = kk * b_x
        store[AY, x, sl, :] = kk * b_y
        store[AZ, x, sl, :] = kk * b_z
        store[D, x, sl, :] = 2.0 - kk * (3.0 * bb + b_x + b_y + b_z)
        store[O, x, sl, :] = jnp.zeros((CHUNK, depth), F32)


def add_source(tables, gathered, store):
    planes, rows, depth = store.shape[1:]
    own, own_rows = planes - 2 * HX, rows - 2 * HY
    groups = gathered.shape[0]
    top = tables.shape[0] - 1
    samples = gathered.shape[1] - top * own
    trace = jnp.concatenate([gathered[g, pl.ds(0, samples), :] for g in range(groups)], 1).astype(F32)
    sensors = trace.shape[1]
    row_at = lax.axis_index("grp") * own_rows - HY + lax.broadcasted_iota(jnp.int32, (rows, sensors), 0)
    distance = jnp.abs(row_at - tables[pl.ds(top, 1), :]).astype(F32)
    band = jnp.maximum(0.0, 1.0 - distance / BAND)
    band = jnp.where((row_at >= 0) & (row_at < own_rows * groups), band, 0.0).astype(BF16)
    slab_at = lax.axis_index("slab")
    weights = [jnp.zeros((own, sensors), F32) for _ in range(3)]
    for i in range(top):
        lat = [gathered[g, pl.ds(samples + i * own, own), :] for g in range(groups)]
        lat = jnp.concatenate(lat, 1).astype(F32)
        for j in range(3):
            weights[j] = weights[j] + jnp.where(tables[pl.ds(i, 1), :] == slab_at + (j - 1), lat, 0.0)
    for x in range(1, planes - 1):
        side, at = divmod(x + own - HX, own)
        outer = (trace * weights[side][at : at + 1]).astype(BF16)
        src = TIME_STEP * lax.dot_general(band, outer, (((1,), (1,)), ((), ())), preferred_element_type=F32)
        later = pl.ds(depth - samples, samples)
        if side == 1:
            store[C, x, :, later] += src
        else:
            store[C, x, :, pl.ds(0, depth - samples)] = jnp.zeros((rows, depth - samples), F32)
            store[C, x, :, later] = src


def taken(given, held, sems):
    copies = [pltpu.make_async_copy(src, dst, sems.at[i]) for i, (src, dst) in enumerate(zip(given, held))]
    for copy in copies:
        copy.start()
    return copies


def own_kernel(*refs):
    given, (p, k, b, c), store = refs[:5], refs[5:9], refs[9]
    held, sems = refs[10:15], refs[15]
    row_behind, row_ahead, own_ahead, tables, gathered = held
    planes, rows, _ = store.shape[1:]
    own, own_rows = planes - 2 * HX, rows - 2 * HY
    low, middle, high = pl.ds(0, HY), pl.ds(HY, own_rows), pl.ds(HY + own_rows, HY)
    here = [store.at[f, pl.ds(HX, own), middle, :] for f in (S, K, B, C)]
    copies = taken(given + (p, k, b, c), held + tuple(here), sems)
    for copy in copies[:3]:
        copy.wait()
    for x in range(own):
        for f in (S, C, K, B):
            store[f, HX + x, low, :] = row_behind[f * own + x].astype(F32)
            store[f, HX + x, high, :] = row_ahead[f * own + x].astype(F32)
    for copy in copies[3:]:
        copy.wait()
    vy_behind = row_behind[4 * own + 1].astype(F32)
    vy_last = own_ahead[4 * own + 1].astype(F32)
    for x in range(own):
        for at, vy in ((HY, vy_behind), (HY + own_rows, vy_last)):
            sl = pl.ds(at, 1)
            store[C, HX + x, sl, :] += TIME_STEP * store[K, HX + x, sl, :] * vy[x : x + 1]
    add_source(tables, gathered, store)

    def one_plane(x, _):
        set_coefficients(store, x)
        return 0

    lax.fori_loop(HX + 1, HX + own, one_plane, 0)
    advance_some(store, 0, True)


def first_round_kernel(*refs):
    given, v, store, to_ahead, to_behind = refs[:6], refs[6], refs[8], refs[9], refs[10]
    held, line, sems = refs[11:17], refs[17], refs[18]
    behind, ahead, corner_behind, corner_ahead, row_behind, row_ahead = held
    planes, rows, _ = store.shape[1:]
    edge = planes - HX
    own, own_rows = planes - 2 * HX, rows - 2 * HY
    low, middle, high = pl.ds(0, HY), pl.ds(HY, own_rows), pl.ds(HY + own_rows, HY)
    copies = taken(given + (v.at[0, own - 1],), held + (line.at[middle, :],), sems)
    sent_ahead, sent_behind = main_planes(own)
    moves = ((behind, corner_behind, sent_ahead, -own), (ahead, corner_ahead, sent_behind, own))
    for copy in copies:
        copy.wait()
    for main, corner, spans, shift in moves:
        units = unit_list(spans)
        for i, (f, x) in enumerate(units):
            parts = ((low, corner[2 * i]), (middle, main[i]), (high, corner[2 * i + 1]))
            for sl, part in parts:
                part = part.astype(F32)
                if f == C:
                    part = part + store[C, x + shift, sl, :]
                store[f, x + shift, sl, :] = part
        _, x, count = spans[1]
        fixed = corner[2 * len(units)].astype(F32)
        for i in range(count):
            store[C, x + shift + i, pl.ds(HY, 1), :] += fixed[i : i + 1]
    line[low, :] = row_behind[4 * own].astype(F32)
    line[high, :] = row_ahead[4 * own].astype(F32)
    at = len(unit_list(sent_ahead))
    vx_parts = ((low, corner_behind[2 * at + 1]), (middle, behind[at]), (high, corner_behind[2 * at + 2]))
    for sl, part in vx_parts:
        store[C, HX, sl, :] += TIME_STEP * store[K, HX, sl, :] * part.astype(F32)
        store[C, edge, sl, :] += TIME_STEP * store[K, edge, sl, :] * line[sl, :]

    def one_plane(i, _):
        set_coefficients(store, jnp.where(i < HX, i + 1, i + edge - HX))
        return 0

    lax.fori_loop(0, 2 * HX - 1, one_plane, 0)
    advance_some(store, 0, False)
    pack_state(store, to_ahead, to_behind, 0)


def inner_kernel(store_i, store, *, done):
    del store_i
    advance_some(store, done, True)


def take_halo(behind, ahead, store, skip):
    planes, rows = store.shape[1:3]
    edge = planes - HX
    sl = pl.ds(skip, rows - 2 * skip)
    for i in range(HX):
        store[S, i, sl, :] = behind[i].astype(F32)
        store[S, edge + i, sl, :] = ahead[i].astype(F32)
    for i in range(1, HX):
        for x, got in ((i, behind), (edge + i - 1, ahead)):
            store[O, x, sl, :] = store[S, x, sl, :] - got[HX + i - 1].astype(F32)


def middle_round_kernel(behind, ahead, store_i, store, to_ahead, to_behind, *, done, skips):
    del store_i
    take_halo(behind, ahead, store, skips[0])
    advance_some(store, done, False)
    pack_state(store, to_ahead, to_behind, skips[1])


def last_round_kernel(behind, ahead, v, store_i, p_out, v_out, store, held, in_sems, out_sems, *, done, skip):
    del store_i
    planes, rows, depth = p_out.shape
    own = pl.ds(HY, rows)

    def reads(x):
        return [pltpu.make_async_copy(v.at[i, x], held.at[i, x], in_sems.at[i, x]) for i in range(3)]

    def writes(x):
        pairs = [(f, v_out.at[i, x]) for i, f in enumerate((A, AX, AY))] + [(AZ, p_out.at[x])]
        return [
            pltpu.make_async_copy(store.at[f, HX + x, own, :], dst, out_sems.at[i, x])
            for i, (f, dst) in enumerate(pairs)
        ]

    def start(x, _):
        for copy in reads(x):
            copy.start()
        return 0

    lax.fori_loop(0, planes, start, 0)
    take_halo(behind, ahead, store, skip)
    advance_some(store, done, False)

    def one_plane(x, _):
        for copy in reads(x):
            copy.wait()
        for r in range(0, rows, CHUNK):
            sl, at = pl.ds(r, CHUNK), pl.ds(HY + r, CHUNK)
            row = lax.broadcasted_iota(jnp.int32, (CHUNK, depth), 0)
            lane = lax.broadcasted_iota(jnp.int32, (CHUNK, depth), 1)
            total = store[O, HX + x, at, :]
            below = store[O, HX + x, pl.ds(HY + r + CHUNK, 1), :]
            y_next = jnp.where(row == CHUNK - 1, below, pltpu.roll(total, CHUNK - 1, 0))
            z_next = jnp.where(lane == depth - 1, 0.0, pltpu.roll(total, depth - 1, 1))
            bb = TIME_STEP * store[B, HX + x, at, :]
            store[A, HX + x, at, :] = held[0, x, sl, :] - bb * (store[O, HX + x + 1, at, :] - total)
            store[AX, HX + x, at, :] = held[1, x, sl, :] - bb * (y_next - total)
            store[AY, HX + x, at, :] = held[2, x, sl, :] - bb * (z_next - total)
            store[AZ, HX + x, at, :] = store[S, HX + x, at, :] - total
        for copy in writes(x):
            copy.start()
        return 0

    lax.fori_loop(0, planes, one_plane, 0)

    def finish(x, _):
        for copy in writes(x):
            copy.wait()
        return 0

    lax.fori_loop(0, planes, finish, 0)


def local(pressure, velocity, stiffness, buoyancy, traces, lateral, routes, ycenter):
    planes, rows, depth = pressure.shape
    wide, tall = planes + 2 * HX, rows + 2 * HY
    store_shape = pltpu.VMEM((FIELDS, wide, tall, depth), F32)
    slabs, groups = lax.axis_size("slab"), lax.axis_size("grp")

    def sent(count, height):
        return jax.ShapeDtypeStruct((count, height, depth), BF16)

    def everyones(copies, axis):
        return lax.all_to_all(copies, axis, split_axis=0, concat_axis=0, tiled=True)

    held, samples = traces.shape
    top = routes.shape[1]
    weights = jnp.transpose(lateral, (1, 2, 0)).reshape(top * planes, held)
    copies = pl.pallas_call(
        sensors_kernel,
        out_shape=jax.ShapeDtypeStruct((slabs, held + top * planes, samples), BF16),
        in_specs=[VM] * 2,
        out_specs=VM,
        compiler_params=params(4),
    )(traces, weights)
    got = everyones(copies, "slab")
    tables = jnp.concatenate([routes.T, ycenter[None]], 0)
    tables = jnp.swapaxes(tables.reshape(top + 1, slabs, groups, held), 1, 2).reshape(top + 1, -1)

    n_rows = 4 * planes
    n_ahead, n_behind = [len(unit_list(spans)) for spans in main_planes(planes)]
    inputs = [pltpu.with_memory_space_constraint(x, pltpu.HBM) for x in (pressure, velocity, stiffness, buoyancy)]
    c, row_ahead, row_behind, plane_ahead, plane_behind = pl.pallas_call(
        pack_kernel,
        out_shape=(
            jax.ShapeDtypeStruct(pressure.shape, F32), sent(n_rows + 2, HY), sent(n_rows + 1, HY),
            sent(n_ahead + 1, rows), sent(n_behind, rows),
        ),
        in_specs=[HBM] * 4,
        out_specs=[VM] * 5,
        scratch_shapes=[pltpu.VMEM((6,) + pressure.shape, F32), pltpu.SemaphoreType.DMA((6, planes))],
        compiler_params=params(24),
    )(*inputs)
    from_behind = passed_along(row_ahead, "grp", 1)
    from_ahead = passed_along(row_behind, "grp", -1)
    got, plane_ahead, plane_behind = lax.optimization_barrier((got, plane_ahead, plane_behind))
    main_behind = passed_along(plane_ahead, "slab", 1)
    main_ahead = passed_along(plane_behind, "slab", -1)

    copies = pl.pallas_call(
        functools.partial(repeat_kernel, own=held),
        out_shape=jax.ShapeDtypeStruct((groups, samples + top * planes, slabs * held), BF16),
        in_specs=[VM],
        out_specs=VM,
        compiler_params=params(8),
    )(got)
    gathered = everyones(copies, "grp")

    corner_ahead, corner_behind = pl.pallas_call(
        corner_kernel,
        out_shape=(sent(2 * n_ahead + 3, HY), sent(2 * n_behind + 1, HY)),
        in_specs=[VM] * 4,
        out_specs=[VM] * 2,
        compiler_params=params(8),
    )(from_behind, from_ahead, row_ahead, row_behind)
    corner_from_behind = passed_along(corner_ahead, "slab", 1)
    corner_from_ahead = passed_along(corner_behind, "slab", -1)

    def in_hbm(*values):
        return [pltpu.with_memory_space_constraint(x, pltpu.HBM) for x in values]

    def copied(given, extra):
        return [pltpu.VMEM(x.shape, x.dtype) for x in given] + [pltpu.SemaphoreType.DMA((len(given) + extra,))]

    given = (from_behind, from_ahead, row_ahead, tables, gathered)
    store = pl.pallas_call(
        own_kernel,
        out_shape=store_shape,
        in_specs=[HBM] * 9,
        out_specs=VM,
        scratch_shapes=copied(given, 4),
        compiler_params=params(14),
    )(*in_hbm(*given), inputs[0], inputs[2], inputs[3], *in_hbm(c))
    given = (main_behind, main_ahead, corner_from_behind, corner_from_ahead, from_behind, from_ahead)
    scratch = copied(given, 1)
    store, plane_ahead, plane_behind = pl.pallas_call(
        first_round_kernel,
        out_shape=(store_shape, sent(2 * HX - 1, tall), sent(2 * HX - 1, tall)),
        in_specs=[HBM] * 7 + [VM],
        out_specs=[VM] * 3,
        input_output_aliases={7: 0},
        scratch_shapes=scratch[:-1] + [pltpu.VMEM((tall, depth), F32), scratch[-1]],
        compiler_params=params(14),
    )(*in_hbm(*given), inputs[1], store)

    def inner(store, done):
        return pl.pallas_call(
            functools.partial(inner_kernel, done=done),
            out_shape=store_shape,
            in_specs=[VM],
            out_specs=VM,
            input_output_aliases={0: 0},
            compiler_params=params(14),
        )(store)

    rounds = STEPS // HX
    skips = [SUB * (HX * r // SUB) for r in range(1, rounds)]
    for r in range(1, rounds - 1):
        from_behind = passed_along(plane_ahead, "slab", 1)
        from_ahead = passed_along(plane_behind, "slab", -1)
        store = inner(store, HX * r)
        height = tall - 2 * skips[r]
        store, plane_ahead, plane_behind = pl.pallas_call(
            functools.partial(middle_round_kernel, done=HX * r, skips=skips[r - 1 : r + 1]),
            out_shape=(store_shape, sent(2 * HX - 1, height), sent(2 * HX - 1, height)),
            in_specs=[VM] * 3,
            out_specs=[VM] * 3,
            input_output_aliases={2: 0},
            compiler_params=params(14),
        )(from_behind, from_ahead, store)
    from_behind = passed_along(plane_ahead, "slab", 1)
    from_ahead = passed_along(plane_behind, "slab", -1)
    store = inner(store, HX * (rounds - 1))
    p_out, v_out, _ = pl.pallas_call(
        functools.partial(last_round_kernel, done=HX * (rounds - 1), skip=skips[-1]),
        out_shape=(
            jax.ShapeDtypeStruct(pressure.shape, F32),
            jax.ShapeDtypeStruct(velocity.shape, F32),
            store_shape,
        ),
        in_specs=[VM, VM, HBM, VM],
        out_specs=[HBM, HBM, VM],
        input_output_aliases={3: 2},
        scratch_shapes=[
            pltpu.VMEM(velocity.shape, F32),
            pltpu.SemaphoreType.DMA((3, planes)),
            pltpu.SemaphoreType.DMA((4, planes)),
        ],
        compiler_params=params(14),
    )(from_behind, from_ahead, inputs[1], store)
    return p_out, v_out


def solution(mesh):
    in_specs = (
        P("slab", "grp", None),
        P(None, "slab", "grp", None),
        P("slab", "grp", None),
        P("slab", "grp", None),
        P(("slab", "grp"), None),
        P(("slab", "grp"), None, None),
        P(),
        P(),
    )
    out_specs = (P("slab", "grp", None), P(None, "slab", "grp", None))
    return jax.shard_map(local, mesh=mesh, in_specs=in_specs, out_specs=out_specs, check_vma=False)
```

```python
import functools

import jax
import jax.numpy as jnp
from jax import lax
from jax.experimental import pallas as pl
from jax.experimental.pallas import tpu as pltpu
from jax.sharding import PartitionSpec as P

TIME_STEP = 0.3
STEPS = 16
HX = 4
HY = 16
BAND = 128.0
LANES = 128
SUB = 8
CHUNK = 32
BLOCK = 2
S, C, K, B, O, A, AX, AY, AZ, D = range(10)
FIELDS = 10
FINE = (C, K)
BF16 = jnp.bfloat16
F32 = jnp.float32
VM = pl.BlockSpec(memory_space=pltpu.VMEM)
HBM = pl.BlockSpec(memory_space=pltpu.HBM)


def passed_along(value, axis, steps):
    count = lax.axis_size(axis)
    first, last = (max(0, -steps), min(count, count - steps))
    return lax.ppermute(value, axis, [(source, source + steps) for source in range(first, last)])


def params(mib):
    return pltpu.CompilerParams(vmem_limit_bytes=mib << 20)


def main_planes(planes):
    ahead = [(f, planes + skip, HX - skip) for f, skip in enumerate((0, 1, 1, 0))]
    behind = [(f, HX, HX - skip) for f, skip in enumerate((0, 1, 1, 1))]
    return ahead, behind


def unit_list(spans):
    return [(f, x) for f, first, count in spans for x in range(first, first + count)]


def rest(value):
    return (value - value.astype(BF16).astype(F32)).astype(BF16)


def pack_kernel(p, v, k, b, c_out, row_ahead, row_behind, plane_ahead, plane_behind, held, sems, out_sems):
    planes, rows, depth = p.shape
    p_e, k_e, b_e, c = (held.at[i] for i in range(3, 7))

    def away(x):
        return pltpu.make_async_copy(c.at[x], c_out.at[x], out_sems.at[x])

    def copies(x):
        pairs = [(v.at[i, x], held.at[i, x]) for i in range(3)]
        pairs = pairs + [(src.at[x], dst.at[x]) for src, dst in ((k, k_e), (p, p_e), (b, b_e))]
        return [pltpu.make_async_copy(src, dst, sems.at[i, x]) for i, (src, dst) in enumerate(pairs)]

    def start(x, _):
        for copy in copies(x):
            copy.start()
        return 0

    lax.fori_loop(0, planes, start, 0)
    fields = (p_e, c, k_e, b_e)

    def one_plane(x, _):
        for copy in copies(x):
            copy.wait()
        prev = jnp.maximum(x - 1, 0)
        for r in range(0, rows, CHUNK):
            sl = pl.ds(r, CHUNK)
            lane = lax.broadcasted_iota(jnp.int32, (CHUNK, depth), 1)
            row = lax.broadcasted_iota(jnp.int32, (CHUNK, depth), 0)
            vx, vy, vz = held[0, x, sl, :], held[1, x, sl, :], held[2, x, sl, :]
            vx_prev = jnp.where(x > 0, held[0, prev, sl, :], 0.0)
            above = jnp.zeros((1, depth), F32) if r == 0 else held[1, x, pl.ds(r - 1, 1), :]
            vy_prev = jnp.where(row == 0, above, pltpu.roll(vy, 1, 0))
            vz_prev = jnp.where(lane == 0, 0.0, pltpu.roll(vz, 1, 1))
            div = (vx - vx_prev) + (vy - vy_prev) + (vz - vz_prev)
            c[x, sl, :] = -TIME_STEP * k_e[x, sl, :] * div
        away(x).start()
        for f, field in enumerate(fields):
            row_ahead[f * planes + x] = field[x, pl.ds(rows - HY, HY), :].astype(BF16)
            row_behind[f * planes + x] = field[x, pl.ds(0, HY), :].astype(BF16)
        return 0

    lax.fori_loop(0, planes, one_plane, 0)
    ahead, behind = main_planes(planes)
    for out, spans in ((plane_ahead, ahead), (plane_behind, behind)):
        for i, (f, x) in enumerate(unit_list(spans)):
            out[i] = fields[f][x - HX].astype(BF16)
    vx_at = len(unit_list(ahead))
    plane_ahead[vx_at] = held[0, planes - 1].astype(BF16)
    for out, first, x in ((plane_ahead, vx_at + 1, planes - 1), (plane_behind, len(unit_list(behind)), 0)):
        for i, f in enumerate(FINE):
            out[first + i] = rest(fields[f][x])
    row_ahead[4 * planes] = held[0, planes - 1, pl.ds(rows - HY, HY), :].astype(BF16)
    row_behind[4 * planes] = held[0, planes - 1, pl.ds(0, HY), :].astype(BF16)
    edge = held[1, :, rows - 1, :]
    row_ahead[4 * planes + 1] = jnp.concatenate([edge, jnp.zeros((HY - planes, depth), F32)], 0).astype(BF16)

    def finish(x, _):
        away(x).wait()
        return 0

    lax.fori_loop(0, planes, finish, 0)


def corner_kernel(behind, ahead, own_ahead, own_behind, to_ahead, to_behind):
    planes = (behind.shape[0] - 2) // 4
    depth = behind.shape[2]
    row = lax.broadcasted_iota(jnp.int32, (HY, depth), 0)
    vy_behind = behind[4 * planes + 1].astype(F32)
    vy_last = own_ahead[4 * planes + 1].astype(F32)
    for out, spans in zip((to_ahead, to_behind), main_planes(planes)):
        units = unit_list(spans)
        deltas = []
        for i, (f, x) in enumerate(units):
            x = x - HX
            out[2 * i] = behind[f * planes + x]
            got = ahead[f * planes + x]
            if f == C:
                got = got.astype(F32)
                fix = TIME_STEP * ahead[K * planes + x].astype(F32) * vy_last[x : x + 1]
                got = jnp.where(row == 0, got + fix, got).astype(BF16)
                near = own_behind[K * planes + x].astype(F32)[:1]
                deltas.append(TIME_STEP * near * vy_behind[x : x + 1])
            out[2 * i + 1] = got
        deltas = jnp.concatenate(deltas + [jnp.zeros((HY - len(deltas), depth), F32)], 0)
        out[2 * len(units)] = deltas.astype(BF16)
    at = len(unit_list(main_planes(planes)[0]))
    to_ahead[2 * at + 1] = behind[4 * planes]
    to_ahead[2 * at + 2] = ahead[4 * planes]


def sensors_kernel(traces_in, lateral_in, copies, traces, lateral, sems):
    for copy in taken((traces_in, lateral_in), (traces, lateral), sems):
        copy.wait()
    own = traces.shape[0]
    for i in range(copies.shape[0]):
        copies[i, pl.ds(0, own), :] = traces[...]
        copies[i, pl.ds(own, lateral.shape[0]), :] = jnp.zeros((lateral.shape[0], copies.shape[2]), BF16)
        copies[i, pl.ds(own, lateral.shape[0]), pl.ds(0, own)] = lateral[...]


def repeat_kernel(got, copies, *, own):
    slabs, height, samples = got.shape
    rows = got[:, :own, :].astype(F32).reshape(slabs * own, samples)
    traces = jnp.transpose(rows).astype(BF16)
    per = LANES // own
    weights = []
    for first in range(0, slabs, per):
        part = jnp.zeros((height - own, samples), F32)
        for i in range(per):
            piece = got[first + i, pl.ds(own, height - own), :].astype(F32)
            part = part + (pltpu.roll(piece, own * i, 1) if i else piece)
        weights.append(part)
    weights = jnp.concatenate(weights, 1).astype(BF16)
    for g in range(copies.shape[0]):
        copies[g, pl.ds(0, samples), :] = traces
        copies[g, pl.ds(samples, height - own), :] = weights


def tile(x, t, h):
    return (x, pl.ds(SUB * t, SUB), pl.ds(LANES * h, LANES))


def advance_planes(s, o, coef, x, count, t0, t1):
    c, a, ax, ay, az, d = coef
    row = lax.broadcasted_iota(jnp.int32, (SUB, LANES), 0)
    lane = lax.broadcasted_iota(jnp.int32, (SUB, LANES), 1)
    halves = range(s.shape[2] // LANES)

    def around(t):
        here = [[s[tile(x + i, t, h)] for h in halves] for i in range(count)]
        up = [[pltpu.roll(v, SUB - 1, 0) for v in q] for q in here]
        down = [[pltpu.roll(v, 1, 0) for v in q] for q in here]
        return here, up, down

    here, up, down = around(t0)
    down_prev = down
    for t in range(t0, t1):
        later, up_next, down_next = around(t + 1) if t + 1 < t1 else (here, up, down)
        before = [s[tile(x - 1, t, h)] for h in halves]
        for i in range(count):
            now = here[i]
            after = here[i + 1] if i + 1 < count else [s[tile(x + count, t, h)] for h in halves]
            right = [pltpu.roll(v, LANES - 1, 1) for v in now] + [jnp.zeros((SUB, LANES), F32)]
            left = [pltpu.roll(v, 1, 1) for v in now]
            for h in halves:
                at = tile(x + i, t, h)
                y_next = jnp.where(row == SUB - 1, up_next[i][h], up[i][h])
                y_prev = jnp.where(row == 0, down_prev[i][h], down[i][h])
                z_next = jnp.where(lane == LANES - 1, right[h + 1], right[h])
                z_prev = left[0] if h == 0 else jnp.where(lane == 0, left[h - 1], left[h])
                moved = a[at] * (after[h] + y_next + z_next) + ax[at] * before[h]
                moved = moved + ay[at] * y_prev + az[at] * z_prev + d[at] * now[h]
                o[at] = moved + (c[at] - o[at])
            before = now
        here, up, down, down_prev = later, up_next, down_next, down


def advance_some(store, done, inner, first_step, end_step):
    planes, rows = store.shape[1:3]
    fields = [store.at[S], store.at[O]]
    coef = [store.at[f] for f in (C, A, AX, AY, AZ, D)]
    edge = planes - HX
    for step in range(first_step, end_step):
        now, then = fields[(step - 1) % 2], fields[step % 2]
        skip = (done + step - 1) // SUB
        t0, t1 = skip, rows // SUB - skip
        if inner:
            inside = planes - 2 * HX - 2 * step
            block = 3 if inside % 3 == 0 else 4 if inside % 4 == 0 else 2
            first, count, stride = HX + step, inside // block, block
        else:
            first, count, stride, block = step, 2, edge - 2 * step, HX

        def some_planes(i, _, now=now, then=then, first=first, stride=stride, block=block, t0=t0, t1=t1):
            advance_planes(now, then, coef, first + i * stride, block, t0, t1)
            return 0

        if count > 0:
            lax.fori_loop(0, count, some_planes, 0)


def pack_state(store, to_ahead, to_behind, skip):
    planes, rows = store.shape[1:3]
    edge = planes - HX
    sl = pl.ds(skip, rows - 2 * skip)
    for depth in range(2, HX + 1):
        for out, x in ((to_behind, HX - 1 + depth), (to_ahead, edge - depth)):
            out[depth - 2] = store[S, x, sl, :].astype(BF16)
            if depth < HX:
                out[HX + depth - 3] = (store[S, x, sl, :] - store[O, x, sl, :]).astype(BF16)


def set_coefficients(store, x):
    rows, depth = store.shape[2:]
    for r in range(0, rows, CHUNK):
        sl = pl.ds(r, CHUNK)
        row = lax.broadcasted_iota(jnp.int32, (CHUNK, depth), 0)
        lane = lax.broadcasted_iota(jnp.int32, (CHUNK, depth), 1)
        kk = TIME_STEP * TIME_STEP * store[K, x, sl, :]
        bb = store[B, x, sl, :]
        b_x = store[B, x - 1, sl, :]
        above = store[B, x, pl.ds(max(r - 1, 0), 1), :]
        b_y = jnp.where(row == 0, above, pltpu.roll(bb, 1, 0))
        b_z = jnp.where(lane == 0, 0.0, pltpu.roll(bb, 1, 1))
        store[A, x, sl, :] = kk * bb
        store[AX, x, sl, :] = kk * b_x
        store[AY, x, sl, :] = kk * b_y
        store[AZ, x, sl, :] = kk * b_z
        store[D, x, sl, :] = 2.0 - kk * (3.0 * bb + b_x + b_y + b_z)
        store[C, x, sl, :] += store[O, x, sl, :]
        store[O, x, sl, :] = jnp.zeros((CHUNK, depth), F32)


def by_group(row, groups, own):
    count = row.shape[1] // own
    per = LANES // own
    lane = lax.broadcasted_iota(jnp.int32, (1, LANES), 1) // own
    order = [t * groups + g for g in range(groups) for t in range(count // groups)]
    parts = []
    for first in range(0, count, per):
        part = jnp.zeros((1, LANES), row.dtype)
        for i in range(per):
            block, at = divmod(order[first + i], per)
            piece = row[:, LANES * block : LANES * (block + 1)]
            shift = own * (i - at) % LANES
            part = jnp.where(lane == i, pltpu.roll(piece, shift, 1) if shift else piece, part)
        parts.append(part)
    return jnp.concatenate(parts, 1)


def put_source(routes, centre, gathered, store, held):
    planes, rows, depth = store.shape[1:]
    own, own_rows = planes - 2 * HX, rows - 2 * HY
    groups = gathered.shape[0]
    top = routes.shape[0]
    samples = gathered.shape[1] - top * own
    trace = jnp.concatenate([gathered[g, pl.ds(0, samples), :] for g in range(groups)], 1).astype(F32)
    sensors = trace.shape[1]
    row_at = lax.axis_index("grp") * own_rows - HY + lax.broadcasted_iota(jnp.int32, (rows, sensors), 0)
    distance = jnp.abs(row_at - by_group(centre[...], groups, held)).astype(F32)
    band = jnp.maximum(0.0, 1.0 - distance / BAND)
    band = jnp.where((row_at >= 0) & (row_at < own_rows * groups), band, 0.0).astype(BF16)
    slab_at = lax.axis_index("slab")
    weights = [jnp.zeros((own, sensors), F32) for _ in range(3)]
    for i in range(top):
        route = by_group(routes[pl.ds(i, 1), :], groups, held)
        lat = [gathered[g, pl.ds(samples + i * own, own), :] for g in range(groups)]
        lat = jnp.concatenate(lat, 1).astype(F32)
        for j in range(3):
            weights[j] = weights[j] + jnp.where(route == slab_at + (j - 1), lat, 0.0)
    for x in range(1, planes - 1):
        side, at = divmod(x + own - HX, own)
        outer = (trace * weights[side][at : at + 1]).astype(BF16)
        src = lax.dot_general(band, outer, (((1,), (1,)), ((), ())), preferred_element_type=F32)
        store[O, x, :, pl.ds(0, depth - samples)] = jnp.zeros((rows, depth - samples), F32)
        store[O, x, :, pl.ds(depth - samples, samples)] = TIME_STEP * src


def taken(given, held, sems):
    copies = [pltpu.make_async_copy(src, dst, sems.at[i]) for i, (src, dst) in enumerate(zip(given, held))]
    for copy in copies:
        copy.start()
    return copies


def own_kernel(*refs, held):
    given, (p, k, b, c, v), store = refs[:6], refs[6:11], refs[11]
    kept, sems = refs[12:18], refs[18]
    routes, centre, gathered, row_behind, row_ahead, own_ahead = kept
    planes, rows, _ = store.shape[1:]
    own, own_rows = planes - 2 * HX, rows - 2 * HY
    low, middle, high = pl.ds(0, HY), pl.ds(HY, own_rows), pl.ds(HY + own_rows, HY)
    here = [store.at[f, pl.ds(HX, own), middle, :] for f in (S, K, B, C)] + [store.at[K, 0, middle, :]]
    copies = taken(given + (p, k, b, c, v.at[0, own - 1]), kept + tuple(here), sems)
    for copy in copies[:3]:
        copy.wait()
    put_source(routes, centre, gathered, store, held)
    for copy in copies[3:]:
        copy.wait()
    for x in range(own):
        for f in (S, C, K, B):
            store[f, HX + x, low, :] = row_behind[f * own + x].astype(F32)
            store[f, HX + x, high, :] = row_ahead[f * own + x].astype(F32)
    store[K, 0, low, :] = row_behind[4 * own].astype(F32)
    store[K, 0, high, :] = row_ahead[4 * own].astype(F32)
    vy_behind = row_behind[4 * own + 1].astype(F32)
    vy_last = own_ahead[4 * own + 1].astype(F32)
    for x in range(own):
        for at, vy in ((HY, vy_behind), (HY + own_rows, vy_last)):
            sl = pl.ds(at, 1)
            store[C, HX + x, sl, :] += TIME_STEP * store[K, HX + x, sl, :] * vy[x : x + 1]

    def one_plane(x, _):
        set_coefficients(store, x)
        return 0

    lax.fori_loop(HX + 1, HX + own, one_plane, 0)
    advance_some(store, 0, True, 1, HX)


def first_round_kernel(*refs):
    given, store, to_ahead, to_behind = refs[:4], refs[5], refs[6], refs[7]
    held, sems = refs[8:12], refs[12]
    behind, ahead, corner_behind, corner_ahead = held
    planes, rows, _ = store.shape[1:]
    edge = planes - HX
    own, own_rows = planes - 2 * HX, rows - 2 * HY
    low, middle, high = pl.ds(0, HY), pl.ds(HY, own_rows), pl.ds(HY + own_rows, HY)
    copies = taken(given, held, sems)
    sent_ahead, sent_behind = main_planes(own)
    moves = ((behind, corner_behind, sent_ahead, -own), (ahead, corner_ahead, sent_behind, own))
    for side, (main, corner, spans, shift) in enumerate(moves):
        copies[side].wait()
        copies[2 + side].wait()
        units = unit_list(spans)
        for i, (f, x) in enumerate(units):
            store[f, x + shift, low, :] = corner[2 * i].astype(F32)
            store[f, x + shift, middle, :] = main[i].astype(F32)
            store[f, x + shift, high, :] = corner[2 * i + 1].astype(F32)
        for i, f in enumerate(FINE):
            first = len(units) + (1 if side == 0 else 0)
            store[f, HX - 1 if side == 0 else edge, middle, :] += main[first + i].astype(F32)
        _, x, count = spans[1]
        fixed = corner[2 * len(units)].astype(F32)
        for i in range(count):
            store[C, x + shift + i, pl.ds(HY, 1), :] += fixed[i : i + 1]
    at = len(unit_list(sent_ahead))
    vx_parts = (
        (low, corner_behind[2 * at + 1].astype(F32)),
        (middle, behind[at].astype(F32)),
        (high, corner_behind[2 * at + 2].astype(F32)),
    )
    for sl, part in vx_parts:
        store[C, HX, sl, :] += TIME_STEP * store[K, HX, sl, :] * part
        store[C, edge, sl, :] += TIME_STEP * store[K, edge, sl, :] * store[K, 0, sl, :]

    def one_plane(i, _):
        set_coefficients(store, jnp.where(i < HX, i + 1, i + edge - HX))
        return 0

    lax.fori_loop(0, 2 * HX - 1, one_plane, 0)
    advance_some(store, 0, False, 1, HX + 1)
    pack_state(store, to_ahead, to_behind, 0)


def inner_kernel(store_i, store, *, done):
    del store_i
    advance_some(store, done, True, 1, HX)


def take_halo(behind, ahead, store, done, skip):
    planes, rows = store.shape[1:3]
    edge = planes - HX
    sl = pl.ds(skip, rows - 2 * skip)
    for depth in range(2, HX + 1):
        for x, got in ((HX - depth, behind), (edge - 1 + depth, ahead)):
            store[S, x, sl, :] = got[depth - 2].astype(F32)
            if depth < HX:
                store[O, x, sl, :] = store[S, x, sl, :] - got[HX + depth - 3].astype(F32)
    coef = [store.at[f] for f in (C, A, AX, AY, AZ, D)]
    t0 = (done - 1) // SUB
    for x in (HX - 1, edge):
        advance_planes(store.at[O], store.at[S], coef, x, 1, t0, rows // SUB - t0)


def middle_round_kernel(behind, ahead, store_i, store, to_ahead, to_behind, *, done, skips):
    del store_i
    take_halo(behind, ahead, store, done, skips[0])
    advance_some(store, done, False, 1, HX + 1)
    pack_state(store, to_ahead, to_behind, skips[1])


def last_round_kernel(behind, ahead, v, store_i, p_out, v_out, store, held, in_sems, out_sems, *, done, skip):
    del store_i
    planes, rows, depth = p_out.shape
    own = pl.ds(HY, rows)

    def reads(x):
        return [pltpu.make_async_copy(v.at[i, x], held.at[i, x], in_sems.at[i, x]) for i in range(3)]

    def velocity_away(x):
        return [pltpu.make_async_copy(held.at[i, x], v_out.at[i, x], out_sems.at[i, x]) for i in range(3)]

    def pressure_away(x):
        return pltpu.make_async_copy(store.at[K, HX + x, own, :], p_out.at[x], out_sems.at[3, x])

    def start(x, _):
        for copy in reads(x):
            copy.start()
        return 0

    lax.fori_loop(0, planes, start, 0)
    take_halo(behind, ahead, store, done, skip)
    advance_some(store, done, False, 1, HX)

    def last_velocity(x, _):
        for copy in reads(x):
            copy.wait()
        for r in range(0, rows, CHUNK):
            sl, at = pl.ds(r, CHUNK), pl.ds(HY + r, CHUNK)
            row = lax.broadcasted_iota(jnp.int32, (CHUNK, depth), 0)
            lane = lax.broadcasted_iota(jnp.int32, (CHUNK, depth), 1)
            total = store[O, HX + x, at, :]
            below = store[O, HX + x, pl.ds(HY + r + CHUNK, 1), :]
            y_next = jnp.where(row == CHUNK - 1, below, pltpu.roll(total, CHUNK - 1, 0))
            z_next = jnp.where(lane == depth - 1, 0.0, pltpu.roll(total, depth - 1, 1))
            bb = TIME_STEP * store[B, HX + x, at, :]
            held[0, x, sl, :] = held[0, x, sl, :] - bb * (store[O, HX + x + 1, at, :] - total)
            held[1, x, sl, :] = held[1, x, sl, :] - bb * (y_next - total)
            held[2, x, sl, :] = held[2, x, sl, :] - bb * (z_next - total)
        for copy in velocity_away(x):
            copy.start()
        return 0

    lax.fori_loop(0, planes, last_velocity, 0)
    advance_some(store, done, False, HX, HX + 1)

    def last_pressure(x, _):
        store[K, HX + x, own, :] = store[S, HX + x, own, :] - store[O, HX + x, own, :]
        pressure_away(x).start()
        return 0

    lax.fori_loop(0, planes, last_pressure, 0)

    def finish(x, _):
        for copy in velocity_away(x):
            copy.wait()
        pressure_away(x).wait()
        return 0

    lax.fori_loop(0, planes, finish, 0)


def local(pressure, velocity, stiffness, buoyancy, traces, lateral, routes, ycenter):
    planes, rows, depth = pressure.shape
    wide, tall = planes + 2 * HX, rows + 2 * HY
    store_shape = pltpu.VMEM((FIELDS, wide, tall, depth), F32)
    slabs, groups = lax.axis_size("slab"), lax.axis_size("grp")

    def sent(count, height):
        return jax.ShapeDtypeStruct((count, height, depth), BF16)

    def everyones(copies, axis):
        return lax.all_to_all(copies, axis, split_axis=0, concat_axis=0, tiled=True)

    def in_hbm(*values):
        return [pltpu.with_memory_space_constraint(x, pltpu.HBM) for x in values]

    def copied(given, extra):
        return [pltpu.VMEM(x.shape, x.dtype) for x in given] + [pltpu.SemaphoreType.DMA((len(given) + extra,))]

    held, samples = traces.shape
    top = routes.shape[1]
    weights = jnp.transpose(lateral, (1, 2, 0)).reshape(top * planes, held)
    copies = pl.pallas_call(
        sensors_kernel,
        out_shape=jax.ShapeDtypeStruct((slabs, held + top * planes, samples), BF16),
        in_specs=[HBM] * 2,
        out_specs=VM,
        scratch_shapes=copied((traces, weights), 0),
        compiler_params=params(4),
    )(*in_hbm(traces, weights))
    got = everyones(copies, "slab")

    n_rows = 4 * planes
    n_ahead, n_behind = [len(unit_list(spans)) for spans in main_planes(planes)]
    inputs = in_hbm(pressure, velocity, stiffness, buoyancy)
    c, row_ahead, row_behind, plane_ahead, plane_behind = pl.pallas_call(
        pack_kernel,
        out_shape=(
            pltpu.HBM(pressure.shape, F32), sent(n_rows + 2, HY), sent(n_rows + 1, HY),
            sent(n_ahead + 1 + len(FINE), rows), sent(n_behind + len(FINE), rows),
        ),
        in_specs=[HBM] * 4,
        out_specs=[HBM] + [VM] * 4,
        scratch_shapes=[
            pltpu.VMEM((7,) + pressure.shape, F32),
            pltpu.SemaphoreType.DMA((6, planes)),
            pltpu.SemaphoreType.DMA((planes,)),
        ],
        compiler_params=params(24),
    )(*inputs)
    from_behind = passed_along(row_ahead, "grp", 1)
    from_ahead = passed_along(row_behind, "grp", -1)
    got, plane_ahead, plane_behind = lax.optimization_barrier((got, plane_ahead, plane_behind))
    main_behind = passed_along(plane_ahead, "slab", 1)
    main_ahead = passed_along(plane_behind, "slab", -1)

    copies = pl.pallas_call(
        functools.partial(repeat_kernel, own=held),
        out_shape=jax.ShapeDtypeStruct((groups, samples + top * planes, slabs * held), BF16),
        in_specs=[VM],
        out_specs=VM,
        compiler_params=params(8),
    )(got)
    gathered = everyones(copies, "grp")

    corner_ahead, corner_behind = pl.pallas_call(
        corner_kernel,
        out_shape=(sent(2 * n_ahead + 3, HY), sent(2 * n_behind + 1, HY)),
        in_specs=[VM] * 4,
        out_specs=[VM] * 2,
        compiler_params=params(8),
    )(from_behind, from_ahead, row_ahead, row_behind)
    corner_from_behind = passed_along(corner_ahead, "slab", 1)
    corner_from_ahead = passed_along(corner_behind, "slab", -1)

    given = (routes.T, ycenter[None], gathered, from_behind, from_ahead, row_ahead)
    store = pl.pallas_call(
        functools.partial(own_kernel, held=held),
        out_shape=store_shape,
        in_specs=[HBM] * 11,
        out_specs=VM,
        scratch_shapes=copied(given, 5),
        compiler_params=params(14),
    )(*in_hbm(*given), inputs[0], inputs[2], inputs[3], *in_hbm(c), inputs[1])
    given = (main_behind, main_ahead, corner_from_behind, corner_from_ahead)
    store, plane_ahead, plane_behind = pl.pallas_call(
        first_round_kernel,
        out_shape=(store_shape, sent(2 * HX - 3, tall), sent(2 * HX - 3, tall)),
        in_specs=[HBM] * 4 + [VM],
        out_specs=[VM] * 3,
        input_output_aliases={4: 0},
        scratch_shapes=copied(given, 0),
        compiler_params=params(14),
    )(*in_hbm(*given), store)

    def inner(store, done):
        return pl.pallas_call(
            functools.partial(inner_kernel, done=done),
            out_shape=store_shape,
            in_specs=[VM],
            out_specs=VM,
            input_output_aliases={0: 0},
            compiler_params=params(14),
        )(store)

    rounds = STEPS // HX
    skips = [SUB * (HX * r // SUB) for r in range(1, rounds)]
    for r in range(1, rounds - 1):
        from_behind = passed_along(plane_ahead, "slab", 1)
        from_ahead = passed_along(plane_behind, "slab", -1)
        store = inner(store, HX * r)
        height = tall - 2 * skips[r]
        store, plane_ahead, plane_behind = pl.pallas_call(
            functools.partial(middle_round_kernel, done=HX * r, skips=skips[r - 1 : r + 1]),
            out_shape=(store_shape, sent(2 * HX - 3, height), sent(2 * HX - 3, height)),
            in_specs=[VM] * 3,
            out_specs=[VM] * 3,
            input_output_aliases={2: 0},
            compiler_params=params(14),
        )(from_behind, from_ahead, store)
    from_behind = passed_along(plane_ahead, "slab", 1)
    from_ahead = passed_along(plane_behind, "slab", -1)
    store = inner(store, HX * (rounds - 1))
    p_out, v_out, _ = pl.pallas_call(
        functools.partial(last_round_kernel, done=HX * (rounds - 1), skip=skips[-1]),
        out_shape=(
            jax.ShapeDtypeStruct(pressure.shape, F32),
            jax.ShapeDtypeStruct(velocity.shape, F32),
            store_shape,
        ),
        in_specs=[VM, VM, HBM, VM],
        out_specs=[HBM, HBM, VM],
        input_output_aliases={3: 2},
        scratch_shapes=[
            pltpu.VMEM(velocity.shape, F32),
            pltpu.SemaphoreType.DMA((3, planes)),
            pltpu.SemaphoreType.DMA((4, planes)),
        ],
        compiler_params=params(14),
    )(from_behind, from_ahead, inputs[1], store)
    return p_out, v_out


def solution(mesh):
    in_specs = (
        P("slab", "grp", None),
        P(None, "slab", "grp", None),
        P("slab", "grp", None),
        P("slab", "grp", None),
        P(("slab", "grp"), None),
        P(("slab", "grp"), None, None),
        P(),
        P(),
    )
    out_specs = (P("slab", "grp", None), P(None, "slab", "grp", None))
    return jax.shard_map(local, mesh=mesh, in_specs=in_specs, out_specs=out_specs, check_vma=False)
```
